32 devices in a mesh: grp: 2 (over x), seq: 8 (over z, y), head: 2 (over core).
Axes of the slice: x: 2, y: 2, z: 4, core: 2. Of those that a mesh axis runs over, the one named last changes fastest.
Arguments:
- q_nope: bfloat16 [8, 128, 128], P('grp', ('seq', 'head')), parts along dimension 0, may hold values from -6 to 6
- q_rope: bfloat16 [8, 128, 64], P('grp', ('seq', 'head')), parts along dimension 0, may hold values from -150 to 150
- w_uk: bfloat16 [128, 128, 512], P(('seq', 'head')), may hold values from -0.5 to 0.5
- w_uv: bfloat16 [128, 512, 128], P(('seq', 'head')), may hold values from -1 to 1
- cache: bfloat16 [8, 4096, 576], P('grp', 'seq'), parts along dimension 0, may hold values from -12 to 12
- lengths: int32 [8], P('grp'), parts along dimension 0, may hold values from 2048 to 4096, as said below
- selected: int32 [8, 8, 32], P('grp'), parts along dimension 0, may hold values from 0 to 63, as said below
Outputs:
- attended: bfloat16 [8, 128, 128], P('grp', ('seq', 'head')), parts along dimension 0
- bounds: float32 [8, 8, 64], P('grp', None, 'seq'), parts along dimension 0
The draws below stay inside these ranges and needn't reach their ends.
There are 2 independent parts, one for each index of `grp`. The reference program is written for one: setup_inputs(seed, part) draws one part's arguments, and reference() takes and returns one part's arrays. A program takes and returns all parts, laid end to end along the dimension named above; an argument that names none is the same for every part. Nothing has to cross between parts.
Inputs may be any that keep to these rules, and one draw needn't show every extreme that they name: `lengths`: some request has exactly 4096 cached tokens; every request has 2048 or more. `selected`: for each request and head group the 32 page numbers are distinct and below ceil(lengths[r] / 64); page 0 and the page of the request's last cached token are always among them.
All inputs are finite; a program needn't handle non-finite values.
Results may differ from the reference program's by a relative error of at most 0.0065.
Values may be sent and summed in bfloat16 or wider, within the bound.
A program may use at most 64 MiB of HBM per device.

```python
import jax
import jax.numpy as jnp
from jax import lax

H = 128
DN = 128
DR = 64
DL = 512
DV = 128
GH = 16
PAGE = 64
SEL = 32
R = 4
NG = 8
PAGES = 64
L = 4096


def shared_lengths(key):
    uniform_len = jax.random.randint(jax.random.fold_in(key, 11), (R,), SEL * PAGE, L + 1)
    longest = jax.random.randint(jax.random.fold_in(key, 12), (), 0, R)
    return jnp.where(jnp.arange(R) == longest, L, uniform_len).astype(jnp.int32)


def draw_lengths(key, part):
    return shared_lengths(key)


def draw_selected(key, part):
    request_len = shared_lengths(key)
    pages_used = (request_len + PAGE - 1) // PAGE
    subkeys = jax.random.split(jax.random.fold_in(key, 13), R * NG)

    def shuffle(subkey):
        return jax.random.permutation(subkey, PAGES)
    shuffled = jax.vmap(shuffle)(subkeys).reshape(R, NG, PAGES).astype(jnp.int32)
    page_number = jnp.arange(PAGES, dtype=jnp.int32)[None, None, :]
    ranking = jnp.where(page_number >= pages_used[:, None, None], shuffled + 2 * PAGES, shuffled)
    ranking = jnp.where(page_number == 0, -2, ranking)
    ranking = jnp.where(page_number == (pages_used - 1)[:, None, None], -1, ranking)
    ordering = jnp.argsort(ranking, axis=-1, stable=True)
    return ordering[:, :, :SEL].astype(jnp.int32)


def draw_cache(key, part):
    anchor = jax.random.fold_in(key, 31)
    latent = jnp.clip(jax.random.normal(jax.random.fold_in(anchor, 2), (R, L, DL), jnp.float32), -6.0, 6.0)
    rotary = jnp.clip(jax.random.normal(jax.random.fold_in(anchor, 3), (R, L, DR), jnp.float32), -6.0, 6.0)
    return jnp.concatenate([latent, rotary], axis=2).astype(jnp.bfloat16)


def draw_q_rope(key, part):
    anchor = jax.random.fold_in(key, 41)
    jitter = jax.random.normal(jax.random.fold_in(anchor, 1), (R, H, DR), jnp.float32)
    values = jnp.clip(jitter, -6.0, 6.0)
    return values.astype(jnp.bfloat16)


def levels(own_key, dims, pieces, low, high):
    def one(position, blocks):
        heights = jax.random.uniform(jax.random.fold_in(jax.random.fold_in(own_key, 6), position), (blocks,), jnp.float32, low / len(pieces), high / len(pieces))
        return jnp.repeat(jnp.exp(heights), dims[position] // blocks).reshape((-1,) + (1,) * (len(dims) - position - 1))

    factor_of = one(*pieces[0])
    for cut in pieces[1:]:
        factor_of = factor_of * one(*cut)
    return factor_of


def scatter_about(rng, shape, scale, most, shards=(), held_as=jnp.bfloat16):
    factor_of = levels(rng, shape, shards, -0.22, 0.18) if shards else 1.0
    values = jax.random.normal(rng, shape, jnp.float32) * scale * factor_of
    return jnp.minimum(jnp.maximum(values, -most), most).astype(held_as)


def setup_inputs(seed: int = 0, part: int = 0) -> dict:
    streams_of = jax.random.split(jax.random.key(seed), 8)
    part_splits = jax.random.split(jax.random.fold_in(streams_of[7], part), 8)
    return {
        "q_nope": scatter_about(part_splits[0], (R, H, DN), 1.0, 6.0, ((1, 16),)),
        "q_rope": draw_q_rope(jax.random.fold_in(jax.random.fold_in(streams_of[7], part), 71), part),
        "w_uk": scatter_about(streams_of[2], (H, DN, DL), DN ** -0.5, 0.5, ((0, 16),)),
        "w_uv": scatter_about(streams_of[3], (H, DL, DV), (DL // 16) ** -0.5, 1.0, ((0, 16),)),
        "cache": draw_cache(jax.random.fold_in(jax.random.fold_in(streams_of[7], part), 71), part),
        "lengths": draw_lengths(jax.random.fold_in(jax.random.fold_in(streams_of[7], part), 71), part),
        "selected": draw_selected(jax.random.fold_in(jax.random.fold_in(streams_of[7], part), 71), part),
    }


def reference(q_nope, q_rope, w_uk, w_uv, cache, lengths, selected):
    softmax_scale = (DN + DR) ** -0.5
    query_latent = jnp.einsum("rhn,hnl->rhl", q_nope.astype(jnp.float32), w_uk.astype(jnp.float32)).astype(jnp.bfloat16)
    absorbed = jnp.concatenate([query_latent, q_rope], axis=2)

    def per_request(inputs):
        query_rows, cache_rows, length, picks = inputs
        token_index = jnp.arange(PAGES * PAGE, dtype=jnp.int32).reshape(PAGES, PAGE)
        live_token = token_index < length
        live_page = live_token[:, 0]
        page_blocks = cache_rows.reshape(PAGES, PAGE, DL + DR).astype(jnp.float32)
        page_low = jnp.min(jnp.where(live_token[..., None], page_blocks, jnp.inf), axis=1)
        page_high = jnp.max(jnp.where(live_token[..., None], page_blocks, -jnp.inf), axis=1)
        page_low = jnp.where(live_page[:, None], page_low, 0.0)
        page_high = jnp.where(live_page[:, None], page_high, 0.0)
        middle = (page_low + page_high) * 0.5
        spread = (page_high - page_low) * 0.5
        query_float = query_rows.astype(jnp.float32)
        head_bound = softmax_scale * (
            jnp.dot(query_float, middle.T, precision=lax.Precision.HIGHEST)
            + jnp.dot(jnp.abs(query_float), spread.T, precision=lax.Precision.HIGHEST))
        group_bound = jnp.max(head_bound.reshape(NG, GH, PAGES), axis=1)
        group_bound = jnp.where(live_page[None, :], group_bound, 0.0)
        chosen = page_blocks[picks]
        chosen_live = live_token[picks]
        grouped = query_float.reshape(NG, GH, DL + DR)
        scores = jnp.einsum("gkd,gspd->gksp", grouped, chosen) * softmax_scale
        scores = jnp.where(chosen_live[:, None], scores, -1e30)
        page_top = jnp.max(scores, axis=3)
        weights = jnp.where(chosen_live[:, None], jnp.exp(scores - page_top[..., None]), 0.0).astype(jnp.bfloat16)
        weights = lax.optimization_barrier(weights).astype(jnp.float32)
        page_total = jnp.sum(weights, axis=3)
        page_weighted = jnp.einsum("gksp,gspl->gksl", weights, chosen[..., :DL])
        top = jnp.max(page_top, axis=2)
        factor = jnp.exp(page_top - top[..., None])
        total = jnp.sum(factor * page_total, axis=2)
        weighted = jnp.sum(factor[..., None] * page_weighted, axis=2)
        latent_out = (weighted / total[..., None]).astype(jnp.bfloat16).reshape(H, DL)
        return latent_out, group_bound

    latent_out, bounds = lax.map(per_request, (absorbed, cache, lengths, selected))
    attended = jnp.einsum("rhl,hlv->rhv", latent_out.astype(jnp.float32), w_uv.astype(jnp.float32)).astype(jnp.bfloat16)
    return (attended, bounds)
```

```python
import functools

import jax
import jax.numpy as jnp
from jax import lax
from jax.experimental import pallas as pl
from jax.experimental.pallas import tpu as pltpu
from jax.sharding import PartitionSpec as P

GH = 16
PAGE = 64
LANES = 128
LOWEST = -1e30
FLOOR = -1e29
NT = (((1,), (1,)), ((), ()))


def kernel(
    n, hc, R, hb, T, DL, D, groups, scale,
    len_ref, qn_ref, qr_ref, sel_ref, wuk_hbm, wuv_hbm, cache_hbm,
    out_ref, bounds_ref,
    wuk, wuv, cache, mine, gq, qf, pen, hi_s, lo_s, so, ro, gb, gbr,
    in_sem, uk_sem, q_send, q_recv, p_send, p_recv, o_send, o_recv, b_send, b_recv,
):
    f32, bf16 = jnp.float32, jnp.bfloat16
    me = lax.axis_index("seq")
    hr = lax.axis_index("head")
    H = n * hb
    DR = D - DL
    KT = DL // LANES
    PER = LANES // DR
    RT = -(-R // PER)
    pages = T // PAGE
    nz = n // 2
    z = lax.div(me, 2)
    y = lax.rem(me, 2)
    mate = me + 1 - 2 * y
    col = lax.rem(y + 1 - hr, 2)
    low_half = 2 * z < nz

    def other(i):
        down = nz - 1 - i
        down = jnp.where(down <= z, down - 1, down)
        up = jnp.where(z <= i, i + 1, i)
        return jnp.where(low_half, down, up)

    others = [other(i) for i in range(nz - 1)]

    load_uk = [
        pltpu.make_async_copy(wuk_hbm.at[h], wuk.at[h], uk_sem.at[h]) for h in range(hb)
    ]
    load_cache = [
        pltpu.make_async_copy(cache_hbm.at[r], cache.at[r], in_sem.at[2 + r]) for r in range(R)
    ]
    load_uv = pltpu.make_async_copy(wuv_hbm, wuv, in_sem.at[1])
    for c in load_uk:
        c.start()

    barrier = pltpu.get_barrier_semaphore()

    @pl.when(hr == 1)
    def _():
        for zt in others:
            for h in range(hc):
                pl.semaphore_signal(barrier, inc=1, device_id={"seq": 2 * zt + y, "head": h})
        pl.semaphore_signal(barrier, inc=1, device_id={"head": 0})

    @pl.when(hr == 0)
    def _():
        for h in range(hc):
            pl.semaphore_signal(barrier, inc=1, device_id={"seq": mate, "head": h})

    def spread(rows, width):
        which = lax.rem(lax.broadcasted_iota(jnp.int32, (R * hb, width), 0), hb)
        return jnp.concatenate(
            [jnp.where(which == h, rows, 0.0).astype(bf16) for h in range(hb)], axis=1
        )

    for t in range(RT):
        parts = [qr_ref[r].astype(f32) for r in range(t * PER, min(R, (t + 1) * PER))]
        parts += [jnp.zeros((hb, DR), f32)] * (PER - len(parts))
        mine[t] = jnp.concatenate(parts, axis=1).astype(bf16)
    qn = jnp.concatenate([qn_ref[r].astype(f32) for r in range(R)], axis=0)
    lhs = spread(qn, qn.shape[1])
    for c in load_uk:
        c.wait()
    for c in load_cache:
        c.start()
    load_uv.start()
    latent = jnp.dot(lhs, wuk[...].reshape(lhs.shape[1], DL), preferred_element_type=f32)
    for r in range(R):
        for k in range(KT):
            mine[RT + r * KT + k] = latent[
                r * hb:(r + 1) * hb, k * LANES:(k + 1) * LANES
            ].astype(bf16)

    pl.semaphore_wait(barrier, nz + 1 - hr)

    def span(c):
        return pl.ds(RT + c * KT, KT) if c else pl.ds(0, RT + KT)

    own = 2 * z + hr

    def query_copy(c, k, seq, head):
        return pltpu.make_async_remote_copy(
            src_ref=mine.at[span(c)], dst_ref=gq.at[own, span(c)],
            send_sem=q_send.at[c, k], recv_sem=q_recv.at[c, own],
            device_id={"seq": seq, "head": head},
        )

    def query_recv(c, j):
        pltpu.make_async_remote_copy(
            src_ref=mine.at[span(c)], dst_ref=gq.at[j, span(c)],
            send_sem=q_send.at[c, 0], recv_sem=q_recv.at[c, j], device_id={"seq": mate},
        ).wait_recv()

    def pass_copy(c, i):
        pair = gq.at[pl.ds(2 * others[i], 2), span(c)]
        return pltpu.make_async_remote_copy(
            src_ref=pair, dst_ref=pair,
            send_sem=p_send.at[c, i], recv_sem=p_recv.at[c, others[i]],
            device_id={"seq": mate, "head": 0},
        )

    direct = []
    for c in range(R):
        for i, zt in enumerate(others):
            cp = query_copy(c, i, 2 * zt + y, 1)
            cp.start()
            direct.append(cp)
        cp = query_copy(c, nz - 1, mate, 0)
        cp.start()
        direct.append(cp)

        @pl.when(hr == 0)
        def _():
            query_copy(c, nz, me, 1).start()

    @pl.when(hr == 1)
    def _():
        gq[own] = mine[...]

    row = lax.broadcasted_iota(jnp.int32, (H, groups), 0)
    block = lax.div(row, hb)
    row_head = ((2 * lax.div(block, 2) + col) * hc + lax.rem(block, 2)) * hb + lax.rem(row, hb)
    hot = lax.div(row_head, GH) == lax.broadcasted_iota(jnp.int32, (H, groups), 1)
    hot_b = jnp.where(hot, 1.0, 0.0).astype(bf16)
    tok = me * T + lax.broadcasted_iota(jnp.int32, (groups, T), 1)
    page_of = lax.div(tok, PAGE)
    tok_col = me * T + lax.broadcasted_iota(jnp.int32, (T, 1), 0)
    page_col = (me * pages + lax.broadcasted_iota(jnp.int32, (pages, 1), 0)) * PAGE
    for r in range(R):
        length = len_ref[r]
        sel = sel_ref[r]
        hit = jnp.zeros((groups, T), f32)
        for k in range(sel.shape[1]):
            hit = jnp.where(sel[:, k:k + 1] == page_of, 1.0, hit)
        hit = jnp.where(tok < length, hit, 0.0)
        mask = jnp.dot(hot_b, hit.astype(bf16), preferred_element_type=f32)
        pen[r] = (1.0 - mask) * LOWEST

    TILE = 128 if T % 128 == 0 else T
    eye = jnp.where(
        lax.broadcasted_iota(jnp.int32, (TILE, TILE), 0)
        == lax.broadcasted_iota(jnp.int32, (TILE, TILE), 1), 1.0, 0.0
    ).astype(bf16)
    for r in range(R):
        length = len_ref[r]
        load_cache[r].wait()
        x = jnp.concatenate(
            [
                lax.dot_general(
                    eye, cache[r, :, t * TILE:(t + 1) * TILE], NT, preferred_element_type=f32
                )
                for t in range(T // TILE)
            ],
            axis=0,
        )
        live = tok_col < length
        low = jnp.min(jnp.where(live, x, jnp.inf).reshape(pages, PAGE, D), axis=1)
        high = jnp.max(jnp.where(live, x, -jnp.inf).reshape(pages, PAGE, D), axis=1)
        live_page = page_col < length
        lo_s[r] = jnp.where(live_page, low, 0.0).astype(bf16)
        hi_s[r] = jnp.where(live_page, high, 0.0).astype(bf16)

    lane = lax.broadcasted_iota(jnp.int32, (H, LANES), 1)
    HALF, GAP = LANES // 2, LANES // 8
    stats = jnp.zeros((H, LANES), f32)

    def out_span(c):
        return pl.ds(0, KT + 1) if c == R - 1 else pl.ds(0, KT)

    def out_copy(c, zt, h, k):
        return pltpu.make_async_remote_copy(
            src_ref=so.at[c, 2 * zt + h, out_span(c)], dst_ref=ro.at[c, me, out_span(c)],
            send_sem=o_send.at[c, k], recv_sem=o_recv.at[c, me],
            device_id={"seq": 2 * zt + col, "head": h},
        )

    def out_recv(c, src):
        pltpu.make_async_remote_copy(
            src_ref=so.at[c, 0, out_span(c)], dst_ref=ro.at[c, src, out_span(c)],
            send_sem=o_send.at[c, 0], recv_sem=o_recv.at[c, src], device_id={"seq": mate},
        ).wait_recv()

    o_copies = []
    for c in range(R):
        @pl.when(hr == 1)
        def _():
            for i in reversed(range(nz - 1)):
                for h in range(hc):
                    query_recv(c, 2 * others[i] + h)
                pass_copy(c, i).start()
            query_recv(c, 2 * z)

        @pl.when(hr == 0)
        def _():
            for h in range(hc):
                query_recv(c, 2 * z + h)
            for i in range(nz - 1):
                pass_copy(c, i).wait_recv()

        at = c % PER * DR
        for j in range(n):
            rows = slice(j * hb, (j + 1) * hb)
            for k in range(KT):
                qf[c, rows, k * LANES:(k + 1) * LANES] = gq[j, RT + c * KT + k].astype(f32)
            qf[c, rows, DL:] = gq[j, c // PER].astype(f32)[:, at:at + DR]
        q = qf[c].astype(bf16)
        s = jnp.dot(q, cache[c], preferred_element_type=f32) * scale + pen[c]
        m = jnp.maximum(jnp.max(s, axis=1, keepdims=True), FLOOR)
        w = jnp.exp(s - m).astype(bf16)
        l = jnp.sum(w.astype(f32), axis=1, keepdims=True)
        o = lax.dot_general(w, cache[c, :DL, :], NT, preferred_element_type=f32)
        stats = jnp.where(lane == c, m, jnp.where(lane == HALF + c, l, stats))
        for j in range(n):
            for k in range(KT):
                so[c, j, k] = o[
                    j * hb:(j + 1) * hb, k * LANES:(k + 1) * LANES
                ].astype(bf16)
        if c == R - 1:
            first = stats.astype(bf16).astype(f32)
            rest = stats - first
            second = rest.astype(bf16).astype(f32)
            third = rest - second
            packed = first + pltpu.roll(second, GAP, 1) + pltpu.roll(third, 2 * GAP, 1)
            for j in range(n):
                so[c, j, KT] = packed[j * hb:(j + 1) * hb].astype(bf16)
        for i, zt in enumerate(others):
            for h in range(hc):
                cp = out_copy(c, zt, h, 2 * i + h)
                cp.start()
                o_copies.append(cp)
        cp = out_copy(c, z, 0, 2 * nz - 2)
        cp.start()
        o_copies.append(cp)

        @pl.when(hr == 0)
        def _():
            out_copy(c, z, 1, 2 * nz - 1).start()

        @pl.when(hr == 1)
        def _():
            ro[c, me] = so[c, 2 * z + 1]

    parts = []
    for r in range(R):
        q = qf[r]
        above = jnp.maximum(q, 0.0).astype(bf16)
        below = jnp.minimum(q, 0.0).astype(bf16)
        parts.append(
            lax.dot_general(above, hi_s[r], NT, preferred_element_type=f32)
            + lax.dot_general(below, lo_s[r], NT, preferred_element_type=f32)
        )
    parts.append(jnp.zeros((H, LANES - R * pages), f32))
    head_bound = jnp.concatenate(parts, axis=1) * scale
    gb[...] = jnp.concatenate(
        [
            jnp.max(jnp.where(hot[:, g:g + 1], head_bound, LOWEST), axis=0, keepdims=True)
            for g in range(groups)
        ],
        axis=0,
    )
    b_copy = pltpu.make_async_remote_copy(
        src_ref=gb, dst_ref=gbr, send_sem=b_send, recv_sem=b_recv, device_id={"head": 1 - hr},
    )
    b_copy.start()
    load_uv.wait()
    b_copy.wait_recv()
    best = jnp.maximum(gb[...], gbr[...])
    page_row = (me * pages + lax.broadcasted_iota(jnp.int32, (groups, pages), 1)) * PAGE
    for r in range(R):
        bounds_ref[r] = jnp.where(
            page_row < len_ref[r], best[:, r * pages:(r + 1) * pages], 0.0
        )

    for c in range(R):
        for k in range(1, n):
            out_recv(c, lax.rem(me + k, n))

        @pl.when(hr == 0)
        def _():
            out_recv(c, me)

    def statistics(b):
        x = ro[R - 1, b, KT].astype(f32)
        return x + pltpu.roll(x, LANES - GAP, 1) + pltpu.roll(x, LANES - 2 * GAP, 1)

    held = [statistics(b) for b in range(n)]
    peak = held[0]
    for b in range(1, n):
        peak = jnp.maximum(peak, held[b])
    shares = [jnp.exp(x - peak) for x in held]
    total = shares[0] * pltpu.roll(held[0], HALF, 1)
    for b in range(1, n):
        total += shares[b] * pltpu.roll(held[b], HALF, 1)
    shares = [x / total for x in shares]
    rows = []
    for r in range(R):
        parts = []
        for k in range(KT):
            acc = jnp.zeros((hb, LANES), f32)
            for b in range(n):
                acc += shares[b][:, r:r + 1] * ro[r, b, k].astype(f32)
            parts.append(acc)
        rows.append(jnp.concatenate(parts, axis=1))
    lhs = spread(jnp.concatenate(rows, axis=0), DL)
    res = jnp.dot(lhs, wuv[...].reshape(lhs.shape[1], wuv.shape[2]), preferred_element_type=f32)
    for r in range(R):
        out_ref[r] = res[r * hb:(r + 1) * hb].astype(bf16)
    for cp in direct + o_copies + [b_copy]:
        cp.wait_send()

    @pl.when(hr == 1)
    def _():
        for c in range(R):
            for i in range(nz - 1):
                pass_copy(c, i).wait_send()

    @pl.when(hr == 0)
    def _():
        for c in range(R):
            query_copy(c, nz, me, 1).wait_send()
            out_copy(c, z, 1, 2 * nz - 1).wait_send()


def local(n, hc, q_nope, q_rope, w_uk, w_uv, cache, lengths, selected):
    R, hb, DN = q_nope.shape
    DL, DV = w_uk.shape[2], w_uv.shape[2]
    T, D = cache.shape[1:]
    groups = selected.shape[1]
    pages = T // PAGE
    H = n * hb
    scale = (DN + q_rope.shape[2]) ** (-0.5)
    f32, bf16 = jnp.float32, jnp.bfloat16
    KT = DL // LANES
    tiles = R * KT - (-R // (LANES // q_rope.shape[2]))
    V = pltpu.VMEM
    vm = pl.BlockSpec(memory_space=pltpu.VMEM)
    hbm = pl.BlockSpec(memory_space=pltpu.HBM)
    dma = pltpu.SemaphoreType.DMA
    return pl.pallas_call(
        functools.partial(kernel, n, hc, R, hb, T, DL, D, groups, scale),
        out_shape=(
            V((R, hb, DV), bf16),
            V((R, groups, pages), f32),
        ),
        in_specs=[pl.BlockSpec(memory_space=pltpu.SMEM), vm, vm, vm, hbm, hbm, hbm],
        out_specs=(vm, vm),
        scratch_shapes=[
            V((hb, DN, DL), bf16),
            V((hb, DL, DV), bf16),
            V((R, D, T), bf16),
            V((tiles, hb, LANES), bf16),
            V((n, tiles, hb, LANES), bf16),
            V((R, H, D), f32),
            V((R, H, T), f32),
            V((R, pages, D), bf16),
            V((R, pages, D), bf16),
            V((R, n, KT + 1, hb, LANES), bf16),
            V((R, n, KT + 1, hb, LANES), bf16),
            V((groups, LANES), f32),
            V((groups, LANES), f32),
            dma((2 + R,)),
            dma((hb,)),
            dma((R, n)), dma((R, n)),
            dma((R, n)), dma((R, n)),
            dma((R, n)), dma((R, n)),
            dma, dma,
        ],
        compiler_params=pltpu.CompilerParams(
            collective_id=0, has_side_effects=True, vmem_limit_bytes=61000 * 1024
        ),
    )(lengths, q_nope, q_rope, selected, w_uk, w_uv, jnp.swapaxes(cache, 1, 2))


def solution(mesh):
    placed = (
        P("grp", ("seq", "head"), None),
        P("grp", ("seq", "head"), None),
        P(("seq", "head"), None, None),
        P(("seq", "head"), None, None),
        P("grp", "seq", None),
        P("grp"),
        P("grp", None, None),
    )
    return jax.shard_map(
        functools.partial(local, mesh.shape["seq"], mesh.shape["head"]),
        mesh=mesh,
        in_specs=placed,
        out_specs=(P("grp", ("seq", "head"), None), P("grp", None, "seq")),
        check_vma=False,
    )
```

```python
import functools

import jax
import jax.numpy as jnp
from jax import lax
from jax.experimental import pallas as pl
from jax.experimental.pallas import tpu as pltpu
from jax.sharding import PartitionSpec as P

GH = 16
PAGE = 64
LANES = 128
LOWEST = -1e30
FLOOR = -1e29
NT = (((1,), (1,)), ((), ()))


def kernel(
    n, hc, R, hb, T, DL, D, groups, scale,
    len_hbm, qn_hbm, qr_hbm, sel_hbm, wuk_hbm, wuv_hbm, cache_hbm,
    out_ref, bounds_ref,
    len_ref, qn_ref, qr_ref, sel_ref, wuk, wuv, cache, mine, gq, qf, pen, hi_s, lo_s, so, ro, gb, gbr,
    arg_sem, in_sem, uk_sem, q_send, q_recv, p_send, p_recv, o_send, o_recv, b_send, b_recv,
):
    f32, bf16 = jnp.float32, jnp.bfloat16
    me = lax.axis_index("seq")
    hr = lax.axis_index("head")
    H = n * hb
    DR = D - DL
    KT = DL // LANES
    PER = LANES // DR
    RT = -(-R // PER)
    pages = T // PAGE
    nz = n // 2
    z = lax.div(me, 2)
    y = lax.rem(me, 2)
    mate = me + 1 - 2 * y
    col = lax.rem(y + 1 - hr, 2)
    low_half = 2 * z < nz

    def other(i):
        down = nz - 1 - i
        down = jnp.where(down <= z, down - 1, down)
        up = jnp.where(z <= i, i + 1, i)
        return jnp.where(low_half, down, up)

    others = [other(i) for i in range(nz - 1)]

    load_uk = [
        pltpu.make_async_copy(wuk_hbm.at[h], wuk.at[h], uk_sem.at[h]) for h in range(hb)
    ]
    load_cache = [
        pltpu.make_async_copy(cache_hbm.at[r], cache.at[r], in_sem.at[2 + r]) for r in range(R)
    ]
    load_uv = pltpu.make_async_copy(wuv_hbm, wuv, in_sem.at[1])
    load_q = [
        pltpu.make_async_copy(qn_hbm, qn_ref, arg_sem.at[0]),
        pltpu.make_async_copy(qr_hbm, qr_ref, arg_sem.at[1]),
    ]
    load_sel = [
        pltpu.make_async_copy(sel_hbm, sel_ref, arg_sem.at[2]),
        pltpu.make_async_copy(len_hbm, len_ref, arg_sem.at[3]),
    ]

    barrier = pltpu.get_barrier_semaphore()

    @pl.when(hr == 1)
    def _():
        for zt in others:
            for h in range(hc):
                pl.semaphore_signal(barrier, inc=1, device_id={"seq": 2 * zt + y, "head": h})
        pl.semaphore_signal(barrier, inc=1, device_id={"head": 0})

    @pl.when(hr == 0)
    def _():
        for h in range(hc):
            pl.semaphore_signal(barrier, inc=1, device_id={"seq": mate, "head": h})

    for c in load_q + load_uk + load_sel:
        c.start()

    def spread(rows, width):
        which = lax.rem(lax.broadcasted_iota(jnp.int32, (R * hb, width), 0), hb)
        return jnp.concatenate(
            [jnp.where(which == h, rows, 0.0).astype(bf16) for h in range(hb)], axis=1
        )

    for c in load_q:
        c.wait()
    for t in range(RT):
        parts = [qr_ref[r].astype(f32) for r in range(t * PER, min(R, (t + 1) * PER))]
        parts += [jnp.zeros((hb, DR), f32)] * (PER - len(parts))
        mine[t] = jnp.concatenate(parts, axis=1).astype(bf16)
    qn = jnp.concatenate([qn_ref[r].astype(f32) for r in range(R)], axis=0)
    lhs = spread(qn, qn.shape[1])
    for c in load_uk:
        c.wait()
    for c in load_cache:
        c.start()
    load_uv.start()
    latent = jnp.dot(lhs, wuk[...].reshape(lhs.shape[1], DL), preferred_element_type=f32)
    for r in range(R):
        for k in range(KT):
            mine[RT + r * KT + k] = latent[
                r * hb:(r + 1) * hb, k * LANES:(k + 1) * LANES
            ].astype(bf16)

    pl.semaphore_wait(barrier, nz + 1 - hr)

    def span(c):
        return pl.ds(RT + c * KT, KT) if c else pl.ds(0, RT + KT)

    own = 2 * z + hr

    def query_copy(c, k, seq, head):
        return pltpu.make_async_remote_copy(
            src_ref=mine.at[span(c)], dst_ref=gq.at[own, span(c)],
            send_sem=q_send.at[c, k], recv_sem=q_recv.at[c, own],
            device_id={"seq": seq, "head": head},
        )

    def query_recv(c, j):
        pltpu.make_async_remote_copy(
            src_ref=mine.at[span(c)], dst_ref=gq.at[j, span(c)],
            send_sem=q_send.at[c, 0], recv_sem=q_recv.at[c, j], device_id={"seq": mate},
        ).wait_recv()

    def pass_copy(c, i):
        pair = gq.at[pl.ds(2 * others[i], 2), span(c)]
        return pltpu.make_async_remote_copy(
            src_ref=pair, dst_ref=pair,
            send_sem=p_send.at[c, i], recv_sem=p_recv.at[c, others[i]],
            device_id={"seq": mate, "head": 0},
        )

    direct = []
    for c in range(R):
        for i in range(nz):
            if i < nz - 1:
                cp = query_copy(c, i, 2 * others[i] + y, 1)
            else:
                cp = query_copy(c, i, mate, 0)
            cp.start()
            direct.append(cp)

    @pl.when(hr == 0)
    def _():
        for c in range(R):
            query_copy(c, nz, me, 1).start()

    @pl.when(hr == 1)
    def _():
        gq[own] = mine[...]

    for c in load_sel:
        c.wait()
    row = lax.broadcasted_iota(jnp.int32, (H, groups), 0)
    block = lax.div(row, hb)
    row_head = ((2 * lax.div(block, 2) + col) * hc + lax.rem(block, 2)) * hb + lax.rem(row, hb)
    hot = lax.div(row_head, GH) == lax.broadcasted_iota(jnp.int32, (H, groups), 1)
    hot_b = jnp.where(hot, 1.0, 0.0).astype(bf16)
    tok = me * T + lax.broadcasted_iota(jnp.int32, (groups, T), 1)
    page_of = lax.div(tok, PAGE)
    tok_col = me * T + lax.broadcasted_iota(jnp.int32, (T, 1), 0)
    page_col = (me * pages + lax.broadcasted_iota(jnp.int32, (pages, 1), 0)) * PAGE
    for r in range(R):
        length = len_ref[r]
        sel = sel_ref[r]
        hit = jnp.zeros((groups, T), f32)
        for k in range(sel.shape[1]):
            hit = jnp.where(sel[:, k:k + 1] == page_of, 1.0, hit)
        hit = jnp.where(tok < length, hit, 0.0)
        mask = jnp.dot(hot_b, hit.astype(bf16), preferred_element_type=f32)
        pen[r] = (1.0 - mask) * LOWEST

    TILE = 128 if T % 128 == 0 else T
    eye = jnp.where(
        lax.broadcasted_iota(jnp.int32, (TILE, TILE), 0)
        == lax.broadcasted_iota(jnp.int32, (TILE, TILE), 1), 1.0, 0.0
    ).astype(bf16)
    for r in range(R):
        length = len_ref[r]
        load_cache[r].wait()
        x = jnp.concatenate(
            [
                lax.dot_general(
                    eye, cache[r, :, t * TILE:(t + 1) * TILE], NT, preferred_element_type=f32
                )
                for t in range(T // TILE)
            ],
            axis=0,
        )
        live = tok_col < length
        low = jnp.min(jnp.where(live, x, jnp.inf).reshape(pages, PAGE, D), axis=1)
        high = jnp.max(jnp.where(live, x, -jnp.inf).reshape(pages, PAGE, D), axis=1)
        live_page = page_col < length
        lo_s[r] = jnp.where(live_page, low, 0.0).astype(bf16)
        hi_s[r] = jnp.where(live_page, high, 0.0).astype(bf16)

    lane = lax.broadcasted_iota(jnp.int32, (H, LANES), 1)
    HALF, GAP = LANES // 2, LANES // 8
    stats = jnp.zeros((H, LANES), f32)

    def out_span(c):
        return pl.ds(0, KT + 1) if c == R - 1 else pl.ds(0, KT)

    def out_copy(c, zt, h):
        return pltpu.make_async_remote_copy(
            src_ref=so.at[c, 2 * zt + h, out_span(c)], dst_ref=ro.at[c, me, out_span(c)],
            send_sem=o_send.at[c, 2 * zt + h], recv_sem=o_recv.at[c, me],
            device_id={"seq": 2 * zt + col, "head": h},
        )

    def away(zt):
        return jnp.logical_or(hr == 0, z != zt)

    def out_recv(c, src):
        pltpu.make_async_remote_copy(
            src_ref=so.at[c, 0, out_span(c)], dst_ref=ro.at[c, src, out_span(c)],
            send_sem=o_send.at[c, 0], recv_sem=o_recv.at[c, src], device_id={"seq": mate},
        ).wait_recv()

    def pass_on(c, i):
        for h in range(hc):
            query_recv(c, 2 * others[i] + h)
        pass_copy(c, i).start()

    o_copies = []
    for c in range(R):
        @pl.when(hr == 1)
        def _():
            for i in reversed(range(nz - 1)):
                pass_on(c, i)
            query_recv(c, 2 * z)

        @pl.when(hr == 0)
        def _():
            for h in range(hc):
                query_recv(c, 2 * z + h)
            for i in range(nz - 1):
                pass_copy(c, i).wait_recv()

        at = c % PER * DR
        for j in range(n):
            rows = slice(j * hb, (j + 1) * hb)
            for k in range(KT):
                qf[c, rows, k * LANES:(k + 1) * LANES] = gq[j, RT + c * KT + k].astype(f32)
            qf[c, rows, DL:] = gq[j, c // PER].astype(f32)[:, at:at + DR]
        q = qf[c].astype(bf16)
        s = jnp.dot(q, cache[c], preferred_element_type=f32) * scale + pen[c]
        m = jnp.maximum(jnp.max(s, axis=1, keepdims=True), FLOOR)
        w = jnp.exp(s - m).astype(bf16)
        l = jnp.sum(w.astype(f32), axis=1, keepdims=True)
        o = lax.dot_general(w, cache[c, :DL, :], NT, preferred_element_type=f32)
        stats = jnp.where(lane == c, m, jnp.where(lane == HALF + c, l, stats))
        for j in range(n):
            for k in range(KT):
                so[c, j, k] = o[
                    j * hb:(j + 1) * hb, k * LANES:(k + 1) * LANES
                ].astype(bf16)
        if c == R - 1:
            first = stats.astype(bf16).astype(f32)
            rest = stats - first
            second = rest.astype(bf16).astype(f32)
            third = rest - second
            packed = first + pltpu.roll(second, GAP, 1) + pltpu.roll(third, 2 * GAP, 1)
            for j in range(n):
                so[c, j, KT] = packed[j * hb:(j + 1) * hb].astype(bf16)
        for zt in range(nz):
            cp = out_copy(c, zt, 0)
            cp.start()
            o_copies.append(cp)

            @pl.when(away(zt))
            def _():
                out_copy(c, zt, 1).start()

        @pl.when(hr == 1)
        def _():
            ro[c, me] = so[c, 2 * z + 1]

    parts = []
    for r in range(R):
        q = qf[r]
        above = jnp.maximum(q, 0.0).astype(bf16)
        below = jnp.minimum(q, 0.0).astype(bf16)
        parts.append(
            lax.dot_general(above, hi_s[r], NT, preferred_element_type=f32)
            + lax.dot_general(below, lo_s[r], NT, preferred_element_type=f32)
        )
    parts.append(jnp.zeros((H, LANES - R * pages), f32))
    head_bound = jnp.concatenate(parts, axis=1) * scale
    gb[...] = jnp.concatenate(
        [
            jnp.max(jnp.where(hot[:, g:g + 1], head_bound, LOWEST), axis=0, keepdims=True)
            for g in range(groups)
        ],
        axis=0,
    )
    b_copy = pltpu.make_async_remote_copy(
        src_ref=gb, dst_ref=gbr, send_sem=b_send, recv_sem=b_recv, device_id={"head": 1 - hr},
    )
    b_copy.start()
    load_uv.wait()
    b_copy.wait_recv()
    best = jnp.maximum(gb[...], gbr[...])
    page_row = (me * pages + lax.broadcasted_iota(jnp.int32, (groups, pages), 1)) * PAGE
    for r in range(R):
        bounds_ref[r] = jnp.where(
            page_row < len_ref[r], best[:, r * pages:(r + 1) * pages], 0.0
        )

    for c in range(R):
        for k in range(1, n):
            out_recv(c, lax.rem(me + k, n))

        @pl.when(hr == 0)
        def _():
            out_recv(c, me)

    def statistics(b):
        x = ro[R - 1, b, KT].astype(f32)
        return x + pltpu.roll(x, LANES - GAP, 1) + pltpu.roll(x, LANES - 2 * GAP, 1)

    held = [statistics(b) for b in range(n)]
    peak = held[0]
    for b in range(1, n):
        peak = jnp.maximum(peak, held[b])
    shares = [jnp.exp(x - peak) for x in held]
    total = shares[0] * pltpu.roll(held[0], HALF, 1)
    for b in range(1, n):
        total += shares[b] * pltpu.roll(held[b], HALF, 1)
    shares = [x / total for x in shares]
    rows = []
    for r in range(R):
        parts = []
        for k in range(KT):
            acc = jnp.zeros((hb, LANES), f32)
            for b in range(n):
                acc += shares[b][:, r:r + 1] * ro[r, b, k].astype(f32)
            parts.append(acc)
        rows.append(jnp.concatenate(parts, axis=1))
    lhs = spread(jnp.concatenate(rows, axis=0), DL)
    res = jnp.dot(lhs, wuv[...].reshape(lhs.shape[1], wuv.shape[2]), preferred_element_type=f32)
    for r in range(R):
        out_ref[r] = res[r * hb:(r + 1) * hb].astype(bf16)
    for cp in direct + o_copies + [b_copy]:
        cp.wait_send()

    @pl.when(hr == 1)
    def _():
        for c in range(R):
            for i in range(nz - 1):
                pass_copy(c, i).wait_send()

    @pl.when(hr == 0)
    def _():
        for c in range(R):
            query_copy(c, nz, me, 1).wait_send()

    for zt in range(nz):
        @pl.when(away(zt))
        def _():
            for c in range(R):
                out_copy(c, zt, 1).wait_send()


def local(n, hc, q_nope, q_rope, w_uk, w_uv, cache, lengths, selected):
    R, hb, DN = q_nope.shape
    DL, DV = w_uk.shape[2], w_uv.shape[2]
    T, D = cache.shape[1:]
    groups = selected.shape[1]
    pages = T // PAGE
    H = n * hb
    scale = (DN + q_rope.shape[2]) ** (-0.5)
    f32, bf16 = jnp.float32, jnp.bfloat16
    KT = DL // LANES
    tiles = R * KT - (-R // (LANES // q_rope.shape[2]))
    V = pltpu.VMEM
    vm = pl.BlockSpec(memory_space=pltpu.VMEM)
    hbm = pl.BlockSpec(memory_space=pltpu.HBM)
    dma = pltpu.SemaphoreType.DMA
    return pl.pallas_call(
        functools.partial(kernel, n, hc, R, hb, T, DL, D, groups, scale),
        out_shape=(
            V((R, hb, DV), bf16),
            V((R, groups, pages), f32),
        ),
        in_specs=[hbm] * 7,
        out_specs=(vm, vm),
        scratch_shapes=[
            pltpu.SMEM(lengths.shape, jnp.int32),
            V(q_nope.shape, bf16),
            V(q_rope.shape, bf16),
            V(selected.shape, jnp.int32),
            V((hb, DN, DL), bf16),
            V((hb, DL, DV), bf16),
            V((R, D, T), bf16),
            V((tiles, hb, LANES), bf16),
            V((n, tiles, hb, LANES), bf16),
            V((R, H, D), f32),
            V((R, H, T), f32),
            V((R, pages, D), bf16),
            V((R, pages, D), bf16),
            V((R, n, KT + 1, hb, LANES), bf16),
            V((R, n, KT + 1, hb, LANES), bf16),
            V((groups, LANES), f32),
            V((groups, LANES), f32),
            dma((4,)),
            dma((2 + R,)),
            dma((hb,)),
            dma((R, n)), dma((R, n)),
            dma((R, n)), dma((R, n)),
            dma((R, n)), dma((R, n)),
            dma, dma,
        ],
        compiler_params=pltpu.CompilerParams(
            collective_id=0, has_side_effects=True, vmem_limit_bytes=61000 * 1024
        ),
    )(lengths, q_nope, q_rope, selected, w_uk, w_uv, jnp.swapaxes(cache, 1, 2))


def solution(mesh):
    placed = (
        P("grp", ("seq", "head"), None),
        P("grp", ("seq", "head"), None),
        P(("seq", "head"), None, None),
        P(("seq", "head"), None, None),
        P("grp", "seq", None),
        P("grp"),
        P("grp", None, None),
    )
    return jax.shard_map(
        functools.partial(local, mesh.shape["seq"], mesh.shape["head"]),
        mesh=mesh,
        in_specs=placed,
        out_specs=(P("grp", ("seq", "head"), None), P("grp", None, "seq")),
        check_vma=False,
    )
```

```python
import functools

import jax
import jax.numpy as jnp
from jax import lax
from jax.experimental import pallas as pl
from jax.experimental.pallas import tpu as pltpu
from jax.sharding import PartitionSpec as P

GH = 16
PAGE = 64
LANES = 128
LOWEST = -1e30
FLOOR = -1e29
NT = (((1,), (1,)), ((), ()))


def kernel(
    n, hc, R, hb, T, DL, D, groups, scale,
    len_hbm, qn_hbm, qr_hbm, sel_hbm, wuk_hbm, wuv_hbm, cache_hbm,
    out_ref, bounds_ref,
    len_ref, qn_ref, qr_ref, sel_ref, wuk, wuv, cache, mine, gq, qf, pen, hi_s, lo_s, so, ro, gb, gbr,
    load_sem, q_send, p_send, o_send, b_send, q_recv, o_recv, b_recv,
):
    f32, bf16 = jnp.float32, jnp.bfloat16
    me = lax.axis_index("seq")
    hr = lax.axis_index("head")
    H = n * hb
    DR = D - DL
    KT = DL // LANES
    PER = LANES // DR
    RT = -(-R // PER)
    pages = T // PAGE
    nz = n // 2
    z = lax.div(me, 2)
    y = lax.rem(me, 2)
    mate = me + 1 - 2 * y
    col = lax.rem(y + 1 - hr, 2)
    low_half = 2 * z < nz

    def other(i):
        down = nz - 1 - i
        down = jnp.where(down <= z, down - 1, down)
        up = jnp.where(z <= i, i + 1, i)
        return jnp.where(low_half, down, up)

    others = [other(i) for i in range(nz - 1)]

    load_uk = [
        pltpu.make_async_copy(wuk_hbm.at[h], wuk.at[h], load_sem.at[0]) for h in range(hb)
    ]
    load_cache = [
        pltpu.make_async_copy(cache_hbm.at[r], cache.at[r], load_sem.at[6 + r]) for r in range(R)
    ]
    load_uv = pltpu.make_async_copy(wuv_hbm, wuv, load_sem.at[1])
    load_q = [
        pltpu.make_async_copy(qn_hbm, qn_ref, load_sem.at[2]),
        pltpu.make_async_copy(qr_hbm, qr_ref, load_sem.at[3]),
    ]
    load_sel = [
        pltpu.make_async_copy(sel_hbm, sel_ref, load_sem.at[4]),
        pltpu.make_async_copy(len_hbm, len_ref, load_sem.at[5]),
    ]

    barrier = pltpu.get_barrier_semaphore()

    @pl.when(hr == 1)
    def _():
        for zt in others:
            for h in range(hc):
                pl.semaphore_signal(barrier, inc=1, device_id={"seq": 2 * zt + y, "head": h})
        pl.semaphore_signal(barrier, inc=1, device_id={"head": 0})

    @pl.when(hr == 0)
    def _():
        for h in range(hc):
            pl.semaphore_signal(barrier, inc=1, device_id={"seq": mate, "head": h})

    for c in load_q + load_uk + load_sel:
        c.start()

    def spread(rows, width):
        which = lax.rem(lax.broadcasted_iota(jnp.int32, (R * hb, width), 0), hb)
        return jnp.concatenate(
            [jnp.where(which == h, rows, 0.0).astype(bf16) for h in range(hb)], axis=1
        )

    for c in load_q:
        c.wait()
    for t in range(RT):
        parts = [qr_ref[r].astype(f32) for r in range(t * PER, min(R, (t + 1) * PER))]
        parts += [jnp.zeros((hb, DR), f32)] * (PER - len(parts))
        mine[t] = jnp.concatenate(parts, axis=1).astype(bf16)
    qn = jnp.concatenate([qn_ref[r].astype(f32) for r in range(R)], axis=0)
    lhs = spread(qn, qn.shape[1])
    pltpu.make_async_copy(wuk_hbm, wuk, load_sem.at[0]).wait()
    for c in load_cache:
        c.start()
    load_uv.start()
    latent = jnp.dot(lhs, wuk[...].reshape(lhs.shape[1], DL), preferred_element_type=f32)
    for r in range(R):
        for k in range(KT):
            mine[RT + r * KT + k] = latent[
                r * hb:(r + 1) * hb, k * LANES:(k + 1) * LANES
            ].astype(bf16)

    pl.semaphore_wait(barrier, nz + 1 - hr)

    def span(c):
        return pl.ds(RT + c * KT, KT) if c else pl.ds(0, RT + KT)

    own = 2 * z + hr

    def query_copy(c, seq, head):
        return pltpu.make_async_remote_copy(
            src_ref=mine.at[span(c)], dst_ref=gq.at[own, span(c)],
            send_sem=q_send, recv_sem=q_recv.at[c, z * head],
            device_id={"seq": seq, "head": head},
        )

    def query_recv(c, slot, blocks):
        ref = gq.at[blocks, span(c)]
        pltpu.make_async_remote_copy(
            src_ref=ref, dst_ref=ref, send_sem=q_send, recv_sem=q_recv.at[c, slot],
            device_id={"seq": mate},
        ).wait_recv()

    def pass_copy(c, i):
        pair = gq.at[pl.ds(2 * others[i], 2), span(c)]
        return pltpu.make_async_remote_copy(
            src_ref=pair, dst_ref=pair, send_sem=p_send, recv_sem=q_recv.at[c, 0],
            device_id={"seq": mate, "head": 0},
        )

    def sent(ref, sem):
        pltpu.make_async_remote_copy(
            src_ref=ref, dst_ref=ref, send_sem=sem, recv_sem=b_recv, device_id={"seq": mate},
        ).wait_send()

    for c in range(R):
        for zt in others:
            query_copy(c, 2 * zt + y, 1).start()
        query_copy(c, mate, 0).start()

        @pl.when(hr == 0)
        def _():
            query_copy(c, me, 1).start()

    @pl.when(hr == 1)
    def _():
        gq[own] = mine[...]

    for c in load_sel:
        c.wait()
    row = lax.broadcasted_iota(jnp.int32, (H, groups), 0)
    block = lax.div(row, hb)
    row_head = ((2 * lax.div(block, 2) + col) * hc + lax.rem(block, 2)) * hb + lax.rem(row, hb)
    hot = lax.div(row_head, GH) == lax.broadcasted_iota(jnp.int32, (H, groups), 1)
    hot_b = jnp.where(hot, 1.0, 0.0).astype(bf16)
    tok = me * T + lax.broadcasted_iota(jnp.int32, (groups, T), 1)
    page_of = lax.div(tok, PAGE)
    tok_col = me * T + lax.broadcasted_iota(jnp.int32, (T, 1), 0)
    page_col = (me * pages + lax.broadcasted_iota(jnp.int32, (pages, 1), 0)) * PAGE
    for r in range(R):
        length = len_ref[r]
        sel = sel_ref[r]
        hit = jnp.zeros((groups, T), f32)
        for k in range(sel.shape[1]):
            hit = jnp.where(sel[:, k:k + 1] == page_of, 1.0, hit)
        hit = jnp.where(tok < length, hit, 0.0)
        mask = jnp.dot(hot_b, hit.astype(bf16), preferred_element_type=f32)
        pen[r] = (1.0 - mask) * LOWEST

    TILE = 128 if T % 128 == 0 else T
    eye = jnp.where(
        lax.broadcasted_iota(jnp.int32, (TILE, TILE), 0)
        == lax.broadcasted_iota(jnp.int32, (TILE, TILE), 1), 1.0, 0.0
    ).astype(bf16)
    for r in range(R):
        length = len_ref[r]
        load_cache[r].wait()
        x = jnp.concatenate(
            [
                lax.dot_general(
                    eye, cache[r, :, t * TILE:(t + 1) * TILE], NT, preferred_element_type=f32
                )
                for t in range(T // TILE)
            ],
            axis=0,
        )
        live = tok_col < length
        low = jnp.min(jnp.where(live, x, jnp.inf).reshape(pages, PAGE, D), axis=1)
        high = jnp.max(jnp.where(live, x, -jnp.inf).reshape(pages, PAGE, D), axis=1)
        live_page = page_col < length
        lo_s[r] = jnp.where(live_page, low, 0.0).astype(bf16)
        hi_s[r] = jnp.where(live_page, high, 0.0).astype(bf16)

    lane = lax.broadcasted_iota(jnp.int32, (H, LANES), 1)
    HALF, GAP = LANES // 2, LANES // 8
    stats = jnp.zeros((H, LANES), f32)

    def out_span(c):
        return pl.ds(c * KT, KT + 1) if c == R - 1 else pl.ds(c * KT, KT)

    def out_copy(c, zt, h):
        return pltpu.make_async_remote_copy(
            src_ref=so.at[2 * zt + h, out_span(c)], dst_ref=ro.at[me, out_span(c)],
            send_sem=o_send, recv_sem=o_recv,
            device_id={"seq": 2 * zt + col, "head": h},
        )

    def away(zt):
        return jnp.logical_or(hr == 0, z != zt)

    for c in range(R):
        @pl.when(hr == 1)
        def _():
            for i in reversed(range(nz - 1)):
                query_recv(c, others[i], pl.ds(2 * others[i], 2))
                pass_copy(c, i).start()
            query_recv(c, z, pl.ds(2 * z, 1))

        @pl.when(hr == 0)
        def _():
            query_recv(c, 0, pl.ds(0, n))

        at = c % PER * DR
        for j in range(n):
            rows = slice(j * hb, (j + 1) * hb)
            for k in range(KT):
                qf[c, rows, k * LANES:(k + 1) * LANES] = gq[j, RT + c * KT + k].astype(f32)
            qf[c, rows, DL:] = gq[j, c // PER].astype(f32)[:, at:at + DR]
        q = qf[c].astype(bf16)
        s = jnp.dot(q, cache[c], preferred_element_type=f32) * scale + pen[c]
        m = jnp.maximum(jnp.max(s, axis=1, keepdims=True), FLOOR)
        w = jnp.exp(s - m).astype(bf16)
        l = jnp.sum(w.astype(f32), axis=1, keepdims=True)
        o = lax.dot_general(w, cache[c, :DL, :], NT, preferred_element_type=f32)
        stats = jnp.where(lane == c, m, jnp.where(lane == HALF + c, l, stats))
        for j in range(n):
            for k in range(KT):
                so[j, c * KT + k] = o[
                    j * hb:(j + 1) * hb, k * LANES:(k + 1) * LANES
                ].astype(bf16)
        if c == R - 1:
            first = stats.astype(bf16).astype(f32)
            rest = stats - first
            second = rest.astype(bf16).astype(f32)
            third = rest - second
            packed = first + pltpu.roll(second, GAP, 1) + pltpu.roll(third, 2 * GAP, 1)
            for j in range(n):
                so[j, R * KT] = packed[j * hb:(j + 1) * hb].astype(bf16)
        for zt in range(nz):
            out_copy(c, zt, 0).start()

            @pl.when(away(zt))
            def _():
                out_copy(c, zt, 1).start()

        @pl.when(hr == 1)
        def _():
            ro[me, out_span(c)] = so[2 * z + 1, out_span(c)]

    parts = []
    for r in range(R):
        q = qf[r]
        above = jnp.maximum(q, 0.0).astype(bf16)
        below = jnp.minimum(q, 0.0).astype(bf16)
        parts.append(
            lax.dot_general(above, hi_s[r], NT, preferred_element_type=f32)
            + lax.dot_general(below, lo_s[r], NT, preferred_element_type=f32)
        )
    parts.append(jnp.zeros((H, LANES - R * pages), f32))
    head_bound = jnp.concatenate(parts, axis=1) * scale
    gb[...] = jnp.concatenate(
        [
            jnp.max(jnp.where(hot[:, g:g + 1], head_bound, LOWEST), axis=0, keepdims=True)
            for g in range(groups)
        ],
        axis=0,
    )
    b_copy = pltpu.make_async_remote_copy(
        src_ref=gb, dst_ref=gbr, send_sem=b_send, recv_sem=b_recv, device_id={"head": 1 - hr},
    )
    b_copy.start()
    load_uv.wait()
    b_copy.wait_recv()
    best = jnp.maximum(gb[...], gbr[...])
    page_row = (me * pages + lax.broadcasted_iota(jnp.int32, (groups, pages), 1)) * PAGE
    for r in range(R):
        bounds_ref[r] = jnp.where(
            page_row < len_ref[r], best[:, r * pages:(r + 1) * pages], 0.0
        )

    def out_wait(count):
        ref = ro.at[pl.ds(0, count)]
        pltpu.make_async_remote_copy(
            src_ref=ref, dst_ref=ref, send_sem=o_send, recv_sem=o_recv, device_id={"seq": mate},
        ).wait_recv()

    pl.when(hr == 0)(lambda: out_wait(n))
    pl.when(hr == 1)(lambda: out_wait(n - 1))

    def statistics(b):
        x = ro[b, R * KT].astype(f32)
        return x + pltpu.roll(x, LANES - GAP, 1) + pltpu.roll(x, LANES - 2 * GAP, 1)

    held = [statistics(b) for b in range(n)]
    peak = held[0]
    for b in range(1, n):
        peak = jnp.maximum(peak, held[b])
    shares = [jnp.exp(x - peak) for x in held]
    total = shares[0] * pltpu.roll(held[0], HALF, 1)
    for b in range(1, n):
        total += shares[b] * pltpu.roll(held[b], HALF, 1)
    shares = [x / total for x in shares]
    rows = []
    for r in range(R):
        parts = []
        for k in range(KT):
            acc = jnp.zeros((hb, LANES), f32)
            for b in range(n):
                acc += shares[b][:, r:r + 1] * ro[b, r * KT + k].astype(f32)
            parts.append(acc)
        rows.append(jnp.concatenate(parts, axis=1))
    lhs = spread(jnp.concatenate(rows, axis=0), DL)
    res = jnp.dot(lhs, wuv[...].reshape(lhs.shape[1], wuv.shape[2]), preferred_element_type=f32)
    for r in range(R):
        out_ref[r] = res[r * hb:(r + 1) * hb].astype(bf16)
    b_copy.wait_send()

    @pl.when(hr == 1)
    def _():
        sent(gq.at[pl.ds(0, nz)], q_send)
        sent(gq.at[pl.ds(0, n - 2)], p_send)
        sent(so.at[pl.ds(0, n - 1)], o_send)

    @pl.when(hr == 0)
    def _():
        sent(gq.at[pl.ds(0, nz + 1)], q_send)
        sent(so, o_send)


def local(n, hc, q_nope, q_rope, w_uk, w_uv, cache, lengths, selected):
    R, hb, DN = q_nope.shape
    DL, DV = w_uk.shape[2], w_uv.shape[2]
    T, D = cache.shape[1:]
    groups = selected.shape[1]
    pages = T // PAGE
    H = n * hb
    scale = (DN + q_rope.shape[2]) ** (-0.5)
    f32, bf16 = jnp.float32, jnp.bfloat16
    KT = DL // LANES
    tiles = R * KT - (-R // (LANES // q_rope.shape[2]))
    V = pltpu.VMEM
    vm = pl.BlockSpec(memory_space=pltpu.VMEM)
    hbm = pl.BlockSpec(memory_space=pltpu.HBM)
    dma = pltpu.SemaphoreType.DMA
    return pl.pallas_call(
        functools.partial(kernel, n, hc, R, hb, T, DL, D, groups, scale),
        out_shape=(
            V((R, hb, DV), bf16),
            V((R, groups, pages), f32),
        ),
        in_specs=[hbm] * 7,
        out_specs=(vm, vm),
        scratch_shapes=[
            pltpu.SMEM(lengths.shape, jnp.int32),
            V(q_nope.shape, bf16),
            V(q_rope.shape, bf16),
            V(selected.shape, jnp.int32),
            V((hb, DN, DL), bf16),
            V((hb, DL, DV), bf16),
            V((R, D, T), bf16),
            V((tiles, hb, LANES), bf16),
            V((n, tiles, hb, LANES), bf16),
            V((R, H, D), f32),
            V((R, H, T), f32),
            V((R, pages, D), bf16),
            V((R, pages, D), bf16),
            V((n, R * KT + 1, hb, LANES), bf16),
            V((n, R * KT + 1, hb, LANES), bf16),
            V((groups, LANES), f32),
            V((groups, LANES), f32),
            dma((6 + R,)),
            dma, dma, dma, dma,
            dma((R, n // 2)),
            dma, dma,
        ],
        compiler_params=pltpu.CompilerParams(
            collective_id=0, has_side_effects=True, vmem_limit_bytes=61000 * 1024
        ),
    )(lengths, q_nope, q_rope, selected, w_uk, w_uv, jnp.swapaxes(cache, 1, 2))


def solution(mesh):
    placed = (
        P("grp", ("seq", "head"), None),
        P("grp", ("seq", "head"), None),
        P(("seq", "head"), None, None),
        P(("seq", "head"), None, None),
        P("grp", "seq", None),
        P("grp"),
        P("grp", None, None),
    )
    return jax.shard_map(
        functools.partial(local, mesh.shape["seq"], mesh.shape["head"]),
        mesh=mesh,
        in_specs=placed,
        out_specs=(P("grp", ("seq", "head"), None), P("grp", None, "seq")),
        check_vma=False,
    )
```

```python
import functools

import jax
import jax.numpy as jnp
from jax import lax
from jax.experimental import pallas as pl
from jax.experimental.pallas import tpu as pltpu
from jax.sharding import PartitionSpec as P

GH = 16
PAGE = 64
LANES = 128
LOWEST = -1e30
FLOOR = -1e29
NT = (((1,), (1,)), ((), ()))


def kernel(
    n, hc, R, hb, T, DL, D, groups, scale,
    len_hbm, qn_hbm, qr_hbm, sel_hbm, wuk_hbm, wuv_hbm, cache_hbm,
    out_ref, bounds_ref,
    len_ref, qn_ref, qr_ref, sel_ref, wuk, wuv, cache, mine, gq, qf, pen, hi_s, lo_s, so, ro, gb, gbr,
    load_sem, q_send, p_send, o_send, b_send, q_recv, o_recv, b_recv,
):
    f32, bf16 = jnp.float32, jnp.bfloat16
    me = lax.axis_index("seq")
    hr = lax.axis_index("head")
    H = n * hb
    DR = D - DL
    KT = DL // LANES
    PER = LANES // DR
    RT = -(-R // PER)
    pages = T // PAGE
    nz = n // 2
    z = lax.div(me, 2)
    y = lax.rem(me, 2)
    mate = me + 1 - 2 * y
    col = lax.rem(y + 1 - hr, 2)
    low_half = 2 * z < nz

    def other(i):
        down = nz - 1 - i
        down = jnp.where(down <= z, down - 1, down)
        up = jnp.where(z <= i, i + 1, i)
        return jnp.where(low_half, down, up)

    others = [other(i) for i in range(nz - 1)]

    load_uk = [
        pltpu.make_async_copy(wuk_hbm.at[h], wuk.at[h], load_sem.at[0]) for h in range(hb)
    ]
    load_cache = [
        pltpu.make_async_copy(cache_hbm.at[r], cache.at[r], load_sem.at[6 + r]) for r in range(R)
    ]
    load_uv = pltpu.make_async_copy(wuv_hbm, wuv, load_sem.at[1])
    load_q = [
        pltpu.make_async_copy(qn_hbm, qn_ref, load_sem.at[2]),
        pltpu.make_async_copy(qr_hbm, qr_ref, load_sem.at[3]),
    ]
    load_sel = [
        pltpu.make_async_copy(sel_hbm, sel_ref, load_sem.at[4]),
        pltpu.make_async_copy(len_hbm, len_ref, load_sem.at[5]),
    ]

    barrier = pltpu.get_barrier_semaphore()

    @pl.when(hr == 1)
    def _():
        for zt in others:
            for h in range(hc):
                pl.semaphore_signal(barrier, inc=1, device_id={"seq": 2 * zt + y, "head": h})
        pl.semaphore_signal(barrier, inc=1, device_id={"head": 0})

    @pl.when(hr == 0)
    def _():
        for h in range(hc):
            pl.semaphore_signal(barrier, inc=1, device_id={"seq": mate, "head": h})

    for c in load_q + load_uk + load_sel:
        c.start()

    def spread(rows, width):
        which = lax.rem(lax.broadcasted_iota(jnp.int32, (R * hb, width), 0), hb)
        return jnp.concatenate(
            [jnp.where(which == h, rows, 0.0).astype(bf16) for h in range(hb)], axis=1
        )

    for c in load_q:
        c.wait()
    for t in range(RT):
        parts = [qr_ref[r].astype(f32) for r in range(t * PER, min(R, (t + 1) * PER))]
        parts += [jnp.zeros((hb, DR), f32)] * (PER - len(parts))
        mine[t] = jnp.concatenate(parts, axis=1).astype(bf16)
    qn = jnp.concatenate([qn_ref[r].astype(f32) for r in range(R)], axis=0)
    lhs = spread(qn, qn.shape[1])
    pltpu.make_async_copy(wuk_hbm, wuk, load_sem.at[0]).wait()
    for c in load_cache:
        c.start()
    load_uv.start()
    latent = jnp.dot(lhs, wuk[...].reshape(lhs.shape[1], DL), preferred_element_type=f32)
    for r in range(R):
        for k in range(KT):
            mine[RT + r * KT + k] = latent[
                r * hb:(r + 1) * hb, k * LANES:(k + 1) * LANES
            ].astype(bf16)

    pl.semaphore_wait(barrier, nz + 1 - hr)

    def span(c):
        return pl.ds(RT + c * KT, KT) if c else pl.ds(0, RT + KT)

    own = 2 * z + hr

    def query_copy(c, seq, head):
        return pltpu.make_async_remote_copy(
            src_ref=mine.at[span(c)], dst_ref=gq.at[own, span(c)],
            send_sem=q_send, recv_sem=q_recv.at[c, z * head],
            device_id={"seq": seq, "head": head},
        )

    def query_recv(c, slot, blocks):
        ref = gq.at[blocks, span(c)]
        pltpu.make_async_remote_copy(
            src_ref=ref, dst_ref=ref, send_sem=q_send, recv_sem=q_recv.at[c, slot],
            device_id={"seq": mate},
        ).wait_recv()

    def pass_copy(c, i):
        pair = gq.at[pl.ds(2 * others[i], 2), span(c)]
        return pltpu.make_async_remote_copy(
            src_ref=pair, dst_ref=pair, send_sem=p_send, recv_sem=q_recv.at[c, 0],
            device_id={"seq": mate, "head": 0},
        )

    def sent(ref, sem):
        pltpu.make_async_remote_copy(
            src_ref=ref, dst_ref=ref, send_sem=sem, recv_sem=b_recv, device_id={"seq": mate},
        ).wait_send()

    for c in range(R):
        for zt in others:
            query_copy(c, 2 * zt + y, 1).start()
        query_copy(c, mate, 0).start()

        @pl.when(hr == 0)
        def _():
            query_copy(c, me, 1).start()

    @pl.when(hr == 1)
    def _():
        gq[own] = mine[...]

    for c in load_sel:
        c.wait()
    row = lax.broadcasted_iota(jnp.int32, (H, groups), 0)
    block = lax.div(row, hb)
    row_head = ((2 * lax.div(block, 2) + col) * hc + lax.rem(block, 2)) * hb + lax.rem(row, hb)
    hot = lax.div(row_head, GH) == lax.broadcasted_iota(jnp.int32, (H, groups), 1)
    hot_b = jnp.where(hot, 1.0, 0.0).astype(bf16)
    tok = me * T + lax.broadcasted_iota(jnp.int32, (groups, T), 1)
    page_of = lax.div(tok, PAGE)
    tok_col = me * T + lax.broadcasted_iota(jnp.int32, (T, 1), 0)
    page_col = (me * pages + lax.broadcasted_iota(jnp.int32, (pages, 1), 0)) * PAGE
    for r in range(R):
        length = len_ref[r]
        sel = sel_ref[r]
        hit = jnp.zeros((groups, T), f32)
        for k in range(sel.shape[1]):
            hit = jnp.where(sel[:, k:k + 1] == page_of, 1.0, hit)
        hit = jnp.where(tok < length, hit, 0.0)
        mask = jnp.dot(hot_b, hit.astype(bf16), preferred_element_type=f32)
        pen[r] = (1.0 - mask) * LOWEST

    TILE = 128 if T % 128 == 0 else T
    eye = jnp.where(
        lax.broadcasted_iota(jnp.int32, (TILE, TILE), 0)
        == lax.broadcasted_iota(jnp.int32, (TILE, TILE), 1), 1.0, 0.0
    ).astype(bf16)
    for r in range(R):
        length = len_ref[r]
        load_cache[r].wait()
        x = jnp.concatenate(
            [
                lax.dot_general(
                    eye, cache[r, :, t * TILE:(t + 1) * TILE], NT, preferred_element_type=f32
                )
                for t in range(T // TILE)
            ],
            axis=0,
        )
        live = tok_col < length
        low = jnp.min(jnp.where(live, x, jnp.inf).reshape(pages, PAGE, D), axis=1)
        high = jnp.max(jnp.where(live, x, -jnp.inf).reshape(pages, PAGE, D), axis=1)
        live_page = page_col < length
        lo_s[r] = jnp.where(live_page, low, 0.0).astype(bf16)
        hi_s[r] = jnp.where(live_page, high, 0.0).astype(bf16)

    lane = lax.broadcasted_iota(jnp.int32, (H, LANES), 1)
    HALF, GAP = LANES // 2, LANES // 8
    stats = jnp.zeros((H, LANES), f32)

    def out_span(c):
        return pl.ds(c * KT, KT + 1) if c == R - 1 else pl.ds(c * KT, KT)

    def out_copy(c, zt, h):
        return pltpu.make_async_remote_copy(
            src_ref=so.at[2 * zt + h, out_span(c)], dst_ref=ro.at[me, out_span(c)],
            send_sem=o_send, recv_sem=o_recv,
            device_id={"seq": 2 * zt + col, "head": h},
        )

    def send_out(c, zt):
        out_copy(c, zt, 0).start()
        pl.when(away(zt))(lambda: out_copy(c, zt, 1).start())

    def away(zt):
        return jnp.logical_or(hr == 0, z != zt)

    for c in range(R):
        @pl.when(hr == 1)
        def _():
            for i in reversed(range(nz - 1)):
                query_recv(c, others[i], pl.ds(2 * others[i], 2))
                pass_copy(c, i).start()
            query_recv(c, z, pl.ds(2 * z, 1))

        @pl.when(hr == 0)
        def _():
            query_recv(c, 0, pl.ds(0, n))

        at = c % PER * DR
        for j in range(n):
            rows = slice(j * hb, (j + 1) * hb)
            for k in range(KT):
                qf[c, rows, k * LANES:(k + 1) * LANES] = gq[j, RT + c * KT + k].astype(f32)
            qf[c, rows, DL:] = gq[j, c // PER].astype(f32)[:, at:at + DR]
        q = qf[c].astype(bf16)
        s = jnp.dot(q, cache[c], preferred_element_type=f32) * scale + pen[c]
        m = jnp.maximum(jnp.max(s, axis=1, keepdims=True), FLOOR)
        w = jnp.exp(s - m).astype(bf16)
        l = jnp.sum(w.astype(f32), axis=1, keepdims=True)
        o = lax.dot_general(w, cache[c, :DL, :], NT, preferred_element_type=f32)
        stats = jnp.where(lane == c, m, jnp.where(lane == HALF + c, l, stats))
        for j in range(n):
            for k in range(KT):
                so[j, c * KT + k] = o[
                    j * hb:(j + 1) * hb, k * LANES:(k + 1) * LANES
                ].astype(bf16)
        if c == R - 1:
            first = stats.astype(bf16).astype(f32)
            rest = stats - first
            second = rest.astype(bf16).astype(f32)
            third = rest - second
            packed = first + pltpu.roll(second, GAP, 1) + pltpu.roll(third, 2 * GAP, 1)
            for j in range(n):
                so[j, R * KT] = packed[j * hb:(j + 1) * hb].astype(bf16)
        send_out(c, 0)
        for zt in range(2, nz):
            send_out(c, zt)
        if c == R - 1:
            for cc in range(R):
                send_out(cc, 1)

        @pl.when(hr == 1)
        def _():
            ro[me, out_span(c)] = so[2 * z + 1, out_span(c)]

    parts = []
    for r in range(R):
        q = qf[r]
        above = jnp.maximum(q, 0.0).astype(bf16)
        below = jnp.minimum(q, 0.0).astype(bf16)
        parts.append(
            lax.dot_general(above, hi_s[r], NT, preferred_element_type=f32)
            + lax.dot_general(below, lo_s[r], NT, preferred_element_type=f32)
        )
    parts.append(jnp.zeros((H, LANES - R * pages), f32))
    head_bound = jnp.concatenate(parts, axis=1) * scale
    gb[...] = jnp.concatenate(
        [
            jnp.max(jnp.where(hot[:, g:g + 1], head_bound, LOWEST), axis=0, keepdims=True)
            for g in range(groups)
        ],
        axis=0,
    )
    b_copy = pltpu.make_async_remote_copy(
        src_ref=gb, dst_ref=gbr, send_sem=b_send, recv_sem=b_recv, device_id={"head": 1 - hr},
    )
    b_copy.start()
    load_uv.wait()
    b_copy.wait_recv()
    best = jnp.maximum(gb[...], gbr[...])
    page_row = (me * pages + lax.broadcasted_iota(jnp.int32, (groups, pages), 1)) * PAGE
    for r in range(R):
        bounds_ref[r] = jnp.where(
            page_row < len_ref[r], best[:, r * pages:(r + 1) * pages], 0.0
        )

    def out_wait(count):
        ref = ro.at[pl.ds(0, count)]
        pltpu.make_async_remote_copy(
            src_ref=ref, dst_ref=ref, send_sem=o_send, recv_sem=o_recv, device_id={"seq": mate},
        ).wait_recv()

    pl.when(hr == 0)(lambda: out_wait(n))
    pl.when(hr == 1)(lambda: out_wait(n - 1))

    def statistics(b):
        x = ro[b, R * KT].astype(f32)
        return x + pltpu.roll(x, LANES - GAP, 1) + pltpu.roll(x, LANES - 2 * GAP, 1)

    held = [statistics(b) for b in range(n)]
    peak = held[0]
    for b in range(1, n):
        peak = jnp.maximum(peak, held[b])
    shares = [jnp.exp(x - peak) for x in held]
    total = shares[0] * pltpu.roll(held[0], HALF, 1)
    for b in range(1, n):
        total += shares[b] * pltpu.roll(held[b], HALF, 1)
    shares = [x / total for x in shares]
    rows = []
    for r in range(R):
        parts = []
        for k in range(KT):
            acc = jnp.zeros((hb, LANES), f32)
            for b in range(n):
                acc += shares[b][:, r:r + 1] * ro[b, r * KT + k].astype(f32)
            parts.append(acc)
        rows.append(jnp.concatenate(parts, axis=1))
    lhs = spread(jnp.concatenate(rows, axis=0), DL)
    res = jnp.dot(lhs, wuv[...].reshape(lhs.shape[1], wuv.shape[2]), preferred_element_type=f32)
    for r in range(R):
        out_ref[r] = res[r * hb:(r + 1) * hb].astype(bf16)
    b_copy.wait_send()

    @pl.when(hr == 1)
    def _():
        sent(gq.at[pl.ds(0, nz)], q_send)
        sent(gq.at[pl.ds(0, n - 2)], p_send)
        sent(so.at[pl.ds(0, n - 1)], o_send)

    @pl.when(hr == 0)
    def _():
        sent(gq.at[pl.ds(0, nz + 1)], q_send)
        sent(so, o_send)


def local(n, hc, q_nope, q_rope, w_uk, w_uv, cache, lengths, selected):
    R, hb, DN = q_nope.shape
    DL, DV = w_uk.shape[2], w_uv.shape[2]
    T, D = cache.shape[1:]
    groups = selected.shape[1]
    pages = T // PAGE
    H = n * hb
    scale = (DN + q_rope.shape[2]) ** (-0.5)
    f32, bf16 = jnp.float32, jnp.bfloat16
    KT = DL // LANES
    tiles = R * KT - (-R // (LANES // q_rope.shape[2]))
    V = pltpu.VMEM
    vm = pl.BlockSpec(memory_space=pltpu.VMEM)
    hbm = pl.BlockSpec(memory_space=pltpu.HBM)
    dma = pltpu.SemaphoreType.DMA
    return pl.pallas_call(
        functools.partial(kernel, n, hc, R, hb, T, DL, D, groups, scale),
        out_shape=(
            V((R, hb, DV), bf16),
            V((R, groups, pages), f32),
        ),
        in_specs=[hbm] * 7,
        out_specs=(vm, vm),
        scratch_shapes=[
            pltpu.SMEM(lengths.shape, jnp.int32),
            V(q_nope.shape, bf16),
            V(q_rope.shape, bf16),
            V(selected.shape, jnp.int32),
            V((hb, DN, DL), bf16),
            V((hb, DL, DV), bf16),
            V((R, D, T), bf16),
            V((tiles, hb, LANES), bf16),
            V((n, tiles, hb, LANES), bf16),
            V((R, H, D), f32),
            V((R, H, T), f32),
            V((R, pages, D), bf16),
            V((R, pages, D), bf16),
            V((n, R * KT + 1, hb, LANES), bf16),
            V((n, R * KT + 1, hb, LANES), bf16),
            V((groups, LANES), f32),
            V((groups, LANES), f32),
            dma((6 + R,)),
            dma, dma, dma, dma,
            dma((R, n // 2)),
            dma, dma,
        ],
        compiler_params=pltpu.CompilerParams(
            collective_id=0, has_side_effects=True, vmem_limit_bytes=61000 * 1024
        ),
    )(lengths, q_nope, q_rope, selected, w_uk, w_uv, jnp.swapaxes(cache, 1, 2))


def solution(mesh):
    placed = (
        P("grp", ("seq", "head"), None),
        P("grp", ("seq", "head"), None),
        P(("seq", "head"), None, None),
        P(("seq", "head"), None, None),
        P("grp", "seq", None),
        P("grp"),
        P("grp", None, None),
    )
    return jax.shard_map(
        functools.partial(local, mesh.shape["seq"], mesh.shape["head"]),
        mesh=mesh,
        in_specs=placed,
        out_specs=(P("grp", ("seq", "head"), None), P("grp", None, "seq")),
        check_vma=False,
    )
```

```python
import functools

import jax
import jax.numpy as jnp
from jax import lax
from jax.experimental import pallas as pl
from jax.experimental.pallas import tpu as pltpu
from jax.sharding import PartitionSpec as P

GH = 16
PAGE = 64
LANES = 128
LOWEST = -1e30
FLOOR = -1e29
NT = (((1,), (1,)), ((), ()))


def kernel(
    n, hc, R, hb, T, DL, D, groups, scale,
    len_hbm, qn_hbm, qr_hbm, sel_hbm, wuk_hbm, wuv_hbm, cache_hbm,
    out_ref, bounds_ref,
    len_ref, qn_ref, qr_ref, sel_ref, wuk, wuv, cache, latents, mine, gq, qf, pen, hi_s, lo_s, so, ro, gb, gbr,
    load_sem, q_send, p_send, o_send, b_send, f_send, q_recv, p_recv, o_recv, b_recv, f_recv,
):
    f32, bf16 = jnp.float32, jnp.bfloat16
    me = lax.axis_index("seq")
    hr = lax.axis_index("head")
    H = n * hb
    DR = D - DL
    KT = DL // LANES
    PER = LANES // DR
    RT = -(-R // PER)
    pages = T // PAGE
    nz = n // 2
    z = lax.div(me, 2)
    y = lax.rem(me, 2)
    mate = me + 1 - 2 * y
    columns = (y, 1 - y)
    low_half = 2 * z < nz

    def other(i):
        down = nz - 1 - i
        down = jnp.where(down <= z, down - 1, down)
        up = jnp.where(z <= i, i + 1, i)
        return jnp.where(low_half, down, up)

    others = [other(i) for i in range(nz - 1)]

    load_uk = [
        pltpu.make_async_copy(wuk_hbm.at[h], wuk.at[h], load_sem.at[0]) for h in range(hb)
    ]
    load_cache = [
        pltpu.make_async_copy(cache_hbm.at[r], cache.at[r], load_sem.at[6 + r]) for r in range(R)
    ]
    load_uv = pltpu.make_async_copy(wuv_hbm, wuv, load_sem.at[1])
    load_q = [
        pltpu.make_async_copy(qn_hbm, qn_ref, load_sem.at[2]),
        pltpu.make_async_copy(qr_hbm, qr_ref, load_sem.at[3]),
    ]
    load_sel = [
        pltpu.make_async_copy(sel_hbm, sel_ref, load_sem.at[4]),
        pltpu.make_async_copy(len_hbm, len_ref, load_sem.at[5]),
    ]

    barrier = pltpu.get_barrier_semaphore()

    @pl.when(hr == 1)
    def _():
        for seq in [2 * zt + y for zt in others] + [mate]:
            for h in range(hc):
                pl.semaphore_signal(barrier, inc=1, device_id={"seq": seq, "head": h})
        pl.semaphore_signal(barrier, inc=1, device_id={"head": 0})

    for c in load_q + load_uk + load_sel:
        c.start()

    def spread(rows, width):
        which = lax.rem(lax.broadcasted_iota(jnp.int32, (R * hb, width), 0), hb)
        return jnp.concatenate(
            [jnp.where(which == h, rows, 0.0).astype(bf16) for h in range(hb)], axis=1
        )

    for c in load_q:
        c.wait()
    for t in range(RT):
        parts = [qr_ref[r].astype(f32) for r in range(t * PER, min(R, (t + 1) * PER))]
        parts += [jnp.zeros((hb, DR), f32)] * (PER - len(parts))
        mine[t] = jnp.concatenate(parts, axis=1).astype(bf16)
    qn = jnp.concatenate([qn_ref[r].astype(f32) for r in range(R)], axis=0)
    lhs = spread(qn, qn.shape[1])
    pltpu.make_async_copy(wuk_hbm, wuk, load_sem.at[0]).wait()
    for c in load_cache:
        c.start()
    load_uv.start()
    latent = jnp.dot(lhs, wuk[...].reshape(lhs.shape[1], DL), preferred_element_type=f32)
    for r in range(R):
        for k in range(KT):
            mine[RT + r * KT + k] = latent[
                r * hb:(r + 1) * hb, k * LANES:(k + 1) * LANES
            ].astype(bf16)

    pl.semaphore_wait(barrier, nz + 1 - hr)

    def span(c):
        return pl.ds(RT + c * KT, KT) if c else pl.ds(0, RT + KT)

    own = 2 * z + hr

    def query_copy(c, side, seq):
        return pltpu.make_async_remote_copy(
            src_ref=mine.at[span(c)], dst_ref=gq.at[side, own, span(c)],
            send_sem=q_send, recv_sem=p_recv.at[c] if side else q_recv.at[c, z],
            device_id={"seq": seq, "head": 1},
        )

    def wait_for(ref, sem):
        pltpu.make_async_remote_copy(
            src_ref=ref, dst_ref=ref, send_sem=q_send, recv_sem=sem, device_id={"seq": mate},
        ).wait_recv()

    def pass_on(c, zt):
        pair = (pl.ds(2 * zt, 2), span(c))
        wait_for(gq.at[(0,) + pair], q_recv.at[c, zt])
        pltpu.make_async_remote_copy(
            src_ref=gq.at[(0,) + pair], dst_ref=gq.at[(1,) + pair],
            send_sem=p_send, recv_sem=p_recv.at[c], device_id={"seq": mate, "head": 1},
        ).start()

    def sent(ref, sem):
        pltpu.make_async_remote_copy(
            src_ref=ref, dst_ref=ref, send_sem=sem, recv_sem=b_recv, device_id={"seq": mate},
        ).wait_send()

    for c in range(R):
        for zt in others:
            query_copy(c, 0, 2 * zt + y).start()
        query_copy(c, 1, mate).start()

        @pl.when(hr == 0)
        def _():
            query_copy(c, 0, me).start()

    @pl.when(hr == 1)
    def _():
        gq[0, own] = mine[...]

    for c in load_sel:
        c.wait()
    def groups_of(side):
        row = lax.broadcasted_iota(jnp.int32, (H, groups), 0)
        block = lax.div(row, hb)
        seq = 2 * lax.div(block, 2) + columns[side]
        head = (seq * hc + lax.rem(block, 2)) * hb + lax.rem(row, hb)
        return lax.div(head, GH) == lax.broadcasted_iota(jnp.int32, (H, groups), 1)

    tok = me * T + lax.broadcasted_iota(jnp.int32, (groups, T), 1)
    page_of = lax.div(tok, PAGE)
    tok_col = me * T + lax.broadcasted_iota(jnp.int32, (T, 1), 0)
    page_col = (me * pages + lax.broadcasted_iota(jnp.int32, (pages, 1), 0)) * PAGE
    HALF, GAP = LANES // 2, LANES // 8

    def masks():
        hot_b = [jnp.where(groups_of(side), 1.0, 0.0).astype(bf16) for side in range(2)]
        for r in range(R):
            length = len_ref[r]
            sel = sel_ref[r]
            hit = jnp.zeros((groups, T), f32)
            for k in range(sel.shape[1]):
                hit = jnp.where(sel[:, k:k + 1] == page_of, 1.0, hit)
            hit = jnp.where(tok < length, hit, 0.0).astype(bf16)
            for side in range(2):
                mask = jnp.dot(hot_b[side], hit, preferred_element_type=f32)
                pen[side, r] = (1.0 - mask) * LOWEST

    def transposed(r):
        TILE = 128 if T % 128 == 0 else T
        eye = jnp.where(
            lax.broadcasted_iota(jnp.int32, (TILE, TILE), 0)
            == lax.broadcasted_iota(jnp.int32, (TILE, TILE), 1), 1.0, 0.0
        ).astype(bf16)
        load_cache[r].wait()
        return jnp.concatenate(
            [
                lax.dot_general(
                    eye, cache[r, :, t * TILE:(t + 1) * TILE], NT, preferred_element_type=f32
                )
                for t in range(T // TILE)
            ],
            axis=0,
        )

    def page_extremes():
        for r in range(R):
            length = len_ref[r]
            x = transposed(r)
            live = tok_col < length
            low = jnp.min(jnp.where(live, x, jnp.inf).reshape(pages, PAGE, D), axis=1)
            high = jnp.max(jnp.where(live, x, -jnp.inf).reshape(pages, PAGE, D), axis=1)
            live_page = page_col < length
            lo_s[r] = jnp.where(live_page, low, 0.0).astype(bf16)
            hi_s[r] = jnp.where(live_page, high, 0.0).astype(bf16)

    def out_span(c):
        return pl.ds(c * KT, KT + 1) if c == R - 1 else pl.ds(c * KT, KT)

    def send_out(side, c, zt):
        def out_copy(h):
            return pltpu.make_async_remote_copy(
                src_ref=so.at[side * n + 2 * zt + h, out_span(c)], dst_ref=ro.at[me, out_span(c)],
                send_sem=o_send, recv_sem=o_recv,
                device_id={"seq": 2 * zt + columns[side], "head": h},
            )

        out_copy(0).start()
        if side:
            out_copy(1).start()
        else:
            @pl.when(z != zt)
            def _():
                out_copy(1).start()

    def fill(side, c):
        at = c % PER * DR
        for j in range(n):
            rows = slice(j * hb, (j + 1) * hb)
            for k in range(KT):
                qf[side, c, rows, k * LANES:(k + 1) * LANES] = gq[
                    side, j, RT + c * KT + k
                ].astype(f32)
            qf[side, c, rows, DL:] = gq[side, j, c // PER].astype(f32)[:, at:at + DR]

    def attend(side, c, stats):
        lane = lax.broadcasted_iota(jnp.int32, (H, LANES), 1)
        fill(side, c)
        q = qf[side, c].astype(bf16)
        s = jnp.dot(q, cache[c], preferred_element_type=f32) * scale + pen[side, c]
        m = jnp.maximum(jnp.max(s, axis=1, keepdims=True), FLOOR)
        w = jnp.exp(s - m).astype(bf16)
        l = jnp.sum(w.astype(f32), axis=1, keepdims=True)
        o = jnp.dot(w, latents[c], preferred_element_type=f32)
        stats = jnp.where(lane == c, m, jnp.where(lane == HALF + c, l, stats))
        for j in range(n):
            for k in range(KT):
                so[side * n + j, c * KT + k] = o[
                    j * hb:(j + 1) * hb, k * LANES:(k + 1) * LANES
                ].astype(bf16)
        if c == R - 1:
            first = stats.astype(bf16).astype(f32)
            rest = stats - first
            second = rest.astype(bf16).astype(f32)
            third = rest - second
            packed = first + pltpu.roll(second, GAP, 1) + pltpu.roll(third, 2 * GAP, 1)
            for j in range(n):
                so[side * n + j, R * KT] = packed[j * hb:(j + 1) * hb].astype(bf16)
        return stats

    def hand_over(side):
        return pltpu.make_async_remote_copy(
            src_ref=gq.at[side], dst_ref=gq.at[side],
            send_sem=f_send.at[side], recv_sem=f_recv.at[side], device_id={"head": 0},
        )

    def find_bounds():
        best = None
        for side in range(2):
            hot = groups_of(side)
            parts = []
            hand_over(side).wait_recv()
            for r in range(R):
                fill(side, r)
                q = qf[side, r]
                above = jnp.maximum(q, 0.0).astype(bf16)
                below = jnp.minimum(q, 0.0).astype(bf16)
                parts.append(
                    lax.dot_general(above, hi_s[r], NT, preferred_element_type=f32)
                    + lax.dot_general(below, lo_s[r], NT, preferred_element_type=f32)
                )
            parts.append(jnp.zeros((H, LANES - R * pages), f32))
            head_bound = jnp.concatenate(parts, axis=1) * scale
            found = jnp.concatenate(
                [
                    jnp.max(
                        jnp.where(hot[:, g:g + 1], head_bound, LOWEST), axis=0, keepdims=True
                    )
                    for g in range(groups)
                ],
                axis=0,
            )
            best = found if best is None else jnp.maximum(best, found)
        gb[...] = best

    b_copy = pltpu.make_async_remote_copy(
        src_ref=gb, dst_ref=gbr, send_sem=b_send, recv_sem=b_recv, device_id={"head": 1},
    )

    @pl.when(hr == 1)
    def _():
        masks()
        for r in range(R):
            latents[r] = transposed(r)[:, :DL].astype(bf16)
        for side in range(2):
            stats = jnp.zeros((H, LANES), f32)
            for c in range(R):
                if side:
                    wait_for(gq.at[1, pl.ds(0, n), span(c)], p_recv.at[c])
                else:
                    for zt in reversed(others):
                        pass_on(c, zt)
                    wait_for(gq.at[0, pl.ds(2 * z, 1), span(c)], q_recv.at[c, z])
                if c == R - 1:
                    hand_over(side).start()
                stats = attend(side, c, stats)
                send_out(side, c, 0)
                for zt in range(1, nz):
                    @pl.when(zt >= z)
                    def _():
                        send_out(side, c, zt)
                if side == 1 and c % 2 == 1:
                    @pl.when(1 < z)
                    def _():
                        send_out(0, c - 1, 1)
                        send_out(0, c, 1)
                if side == 0:
                    ro[me, out_span(c)] = so[2 * z + 1, out_span(c)]
        for sd in (1,):
            for cc in range(R):
                for zt in (1,):
                    @pl.when(zt < z)
                    def _():
                        send_out(sd, cc, zt)
        for sd in (0, 1):
            for cc in range(R):
                for zt in range(2, nz):
                    @pl.when(zt < z)
                    def _():
                        send_out(sd, cc, zt)
        b_copy.wait_recv()

    @pl.when(hr == 0)
    def _():
        page_extremes()
        find_bounds()
        b_copy.start()
        gbr[...] = gb[...]

    load_uv.wait()
    page_row = (me * pages + lax.broadcasted_iota(jnp.int32, (groups, pages), 1)) * PAGE
    best = gbr[...]
    for r in range(R):
        bounds_ref[r] = jnp.where(
            page_row < len_ref[r], best[:, r * pages:(r + 1) * pages], 0.0
        )

    def out_wait(count):
        ref = ro.at[pl.ds(0, count)]
        pltpu.make_async_remote_copy(
            src_ref=ref, dst_ref=ref, send_sem=o_send, recv_sem=o_recv, device_id={"seq": mate},
        ).wait_recv()

    pl.when(hr == 0)(lambda: out_wait(n))
    pl.when(hr == 1)(lambda: out_wait(n - 1))

    def statistics(b):
        x = ro[b, R * KT].astype(f32)
        return x + pltpu.roll(x, LANES - GAP, 1) + pltpu.roll(x, LANES - 2 * GAP, 1)

    held = [statistics(b) for b in range(n)]
    peak = held[0]
    for b in range(1, n):
        peak = jnp.maximum(peak, held[b])
    shares = [jnp.exp(x - peak) for x in held]
    total = shares[0] * pltpu.roll(held[0], HALF, 1)
    for b in range(1, n):
        total += shares[b] * pltpu.roll(held[b], HALF, 1)
    shares = [x / total for x in shares]
    rows = []
    for r in range(R):
        parts = []
        for k in range(KT):
            acc = jnp.zeros((hb, LANES), f32)
            for b in range(n):
                acc += shares[b][:, r:r + 1] * ro[b, r * KT + k].astype(f32)
            parts.append(acc)
        rows.append(jnp.concatenate(parts, axis=1))
    lhs = spread(jnp.concatenate(rows, axis=0), DL)
    res = jnp.dot(lhs, wuv[...].reshape(lhs.shape[1], wuv.shape[2]), preferred_element_type=f32)
    for r in range(R):
        out_ref[r] = res[r * hb:(r + 1) * hb].astype(bf16)

    @pl.when(hr == 1)
    def _():
        for side in range(2):
            hand_over(side).wait_send()
        sent(gq.at[0, pl.ds(0, nz)], q_send)
        sent(gq.at[0, pl.ds(0, n - 2)], p_send)
        sent(so.at[pl.ds(0, 2 * n - 1)], o_send)

    @pl.when(hr == 0)
    def _():
        b_copy.wait_send()
        sent(gq.at[0, pl.ds(0, nz + 1)], q_send)


def local(n, hc, q_nope, q_rope, w_uk, w_uv, cache, lengths, selected):
    R, hb, DN = q_nope.shape
    DL, DV = w_uk.shape[2], w_uv.shape[2]
    T, D = cache.shape[1:]
    groups = selected.shape[1]
    pages = T // PAGE
    H = n * hb
    scale = (DN + q_rope.shape[2]) ** (-0.5)
    f32, bf16 = jnp.float32, jnp.bfloat16
    KT = DL // LANES
    tiles = R * KT - (-R // (LANES // q_rope.shape[2]))
    V = pltpu.VMEM
    vm = pl.BlockSpec(memory_space=pltpu.VMEM)
    hbm = pl.BlockSpec(memory_space=pltpu.HBM)
    dma = pltpu.SemaphoreType.DMA
    return pl.pallas_call(
        functools.partial(kernel, n, hc, R, hb, T, DL, D, groups, scale),
        out_shape=(
            V((R, hb, DV), bf16),
            V((R, groups, pages), f32),
        ),
        in_specs=[hbm] * 7,
        out_specs=(vm, vm),
        scratch_shapes=[
            pltpu.SMEM(lengths.shape, jnp.int32),
            V(q_nope.shape, bf16),
            V(q_rope.shape, bf16),
            V(selected.shape, jnp.int32),
            V((hb, DN, DL), bf16),
            V((hb, DL, DV), bf16),
            V((R, D, T), bf16),
            V((R, T, DL), bf16),
            V((tiles, hb, LANES), bf16),
            V((2, n, tiles, hb, LANES), bf16),
            V((2, R, H, D), f32),
            V((2, R, H, T), f32),
            V((R, pages, D), bf16),
            V((R, pages, D), bf16),
            V((2 * n, R * KT + 1, hb, LANES), bf16),
            V((n, R * KT + 1, hb, LANES), bf16),
            V((groups, LANES), f32),
            V((groups, LANES), f32),
            dma((6 + R,)),
            dma, dma, dma, dma, dma((2,)),
            dma((R, n // 2)),
            dma((R,)),
            dma, dma, dma((2,)),
        ],
        compiler_params=pltpu.CompilerParams(
            collective_id=0, has_side_effects=True, vmem_limit_bytes=61000 * 1024
        ),
    )(lengths, q_nope, q_rope, selected, w_uk, w_uv, jnp.swapaxes(cache, 1, 2))


def solution(mesh):
    placed = (
        P("grp", ("seq", "head"), None),
        P("grp", ("seq", "head"), None),
        P(("seq", "head"), None, None),
        P(("seq", "head"), None, None),
        P("grp", "seq", None),
        P("grp"),
        P("grp", None, None),
    )
    return jax.shard_map(
        functools.partial(local, mesh.shape["seq"], mesh.shape["head"]),
        mesh=mesh,
        in_specs=placed,
        out_specs=(P("grp", ("seq", "head"), None), P("grp", None, "seq")),
        check_vma=False,
    )
```

```python
import functools

import jax
import jax.numpy as jnp
from jax import lax
from jax.experimental import pallas as pl
from jax.experimental.pallas import tpu as pltpu
from jax.sharding import PartitionSpec as P

GH = 16
PAGE = 64
LANES = 128
LOWEST = -1e30
FLOOR = -1e29
NT = (((1,), (1,)), ((), ()))


def kernel(
    n, hc, R, hb, T, DL, D, groups, scale,
    len_hbm, qn_hbm, qr_hbm, sel_hbm, wuk_hbm, wuv_hbm, cache_hbm,
    out_ref, bounds_ref,
    len_ref, qn_ref, qr_ref, sel_ref, wuk, wuv, cache, latents, mine, gq, qf, pen, hi_s, lo_s, so, ro, gb, gbr,
    load_sem, q_send, p_send, o_send, b_send, f_send, q_recv, p_recv, o_recv, b_recv, f_recv,
):
    f32, bf16 = jnp.float32, jnp.bfloat16
    me = lax.axis_index("seq")
    hr = lax.axis_index("head")
    H = n * hb
    DR = D - DL
    KT = DL // LANES
    PER = LANES // DR
    RT = -(-R // PER)
    pages = T // PAGE
    nz = n // 2
    z = lax.div(me, 2)
    y = lax.rem(me, 2)
    mate = me + 1 - 2 * y
    columns = (y, 1 - y)
    low_half = 2 * z < nz

    def other(i):
        down = nz - 1 - i
        down = jnp.where(down <= z, down - 1, down)
        up = jnp.where(z <= i, i + 1, i)
        return jnp.where(low_half, down, up)

    others = [other(i) for i in range(nz - 1)]

    load_uk = [
        pltpu.make_async_copy(wuk_hbm.at[h], wuk.at[h], load_sem.at[0]) for h in range(hb)
    ]
    load_cache = [
        pltpu.make_async_copy(cache_hbm.at[r], cache.at[r], load_sem.at[6]) for r in range(R)
    ]
    load_uv = pltpu.make_async_copy(wuv_hbm, wuv, load_sem.at[1])
    load_q = [
        pltpu.make_async_copy(qn_hbm, qn_ref, load_sem.at[2]),
        pltpu.make_async_copy(qr_hbm, qr_ref, load_sem.at[3]),
    ]
    load_sel = [
        pltpu.make_async_copy(sel_hbm, sel_ref, load_sem.at[4]),
        pltpu.make_async_copy(len_hbm, len_ref, load_sem.at[5]),
    ]

    barrier = pltpu.get_barrier_semaphore()

    @pl.when(hr == 1)
    def _():
        for seq in [2 * zt + y for zt in others] + [mate]:
            for h in range(hc):
                pl.semaphore_signal(barrier, inc=1, device_id={"seq": seq, "head": h})
        pl.semaphore_signal(barrier, inc=1, device_id={"head": 0})

    for c in load_q + load_uk + load_sel:
        c.start()

    def spread(rows, width):
        which = lax.rem(lax.broadcasted_iota(jnp.int32, (R * hb, width), 0), hb)
        return jnp.concatenate(
            [jnp.where(which == h, rows, 0.0).astype(bf16) for h in range(hb)], axis=1
        )

    for c in load_q:
        c.wait()
    for t in range(RT):
        parts = [qr_ref[r].astype(f32) for r in range(t * PER, min(R, (t + 1) * PER))]
        parts += [jnp.zeros((hb, DR), f32)] * (PER - len(parts))
        mine[t] = jnp.concatenate(parts, axis=1).astype(bf16)
    qn = jnp.concatenate([qn_ref[r].astype(f32) for r in range(R)], axis=0)
    lhs = spread(qn, qn.shape[1])
    pltpu.make_async_copy(wuk_hbm, wuk, load_sem.at[0]).wait()
    for c in load_cache:
        c.start()
    load_uv.start()
    latent = jnp.dot(lhs, wuk[...].reshape(lhs.shape[1], DL), preferred_element_type=f32)
    for r in range(R):
        for k in range(KT):
            mine[RT + r * KT + k] = latent[
                r * hb:(r + 1) * hb, k * LANES:(k + 1) * LANES
            ].astype(bf16)

    pl.semaphore_wait(barrier, nz + 1 - hr)

    def span(c):
        return pl.ds(RT + c * KT, KT) if c else pl.ds(0, RT + KT)

    own = 2 * z + hr

    def query_copy(c, side, seq):
        return pltpu.make_async_remote_copy(
            src_ref=mine.at[span(c)], dst_ref=gq.at[side, own, span(c)],
            send_sem=q_send, recv_sem=p_recv.at[c] if side else q_recv.at[c, z],
            device_id={"seq": seq, "head": 1},
        )

    def wait_for(ref, sem):
        pltpu.make_async_remote_copy(
            src_ref=ref, dst_ref=ref, send_sem=q_send, recv_sem=sem, device_id={"seq": mate},
        ).wait_recv()

    def pass_on(c, zt):
        pair = (pl.ds(2 * zt, 2), span(c))
        wait_for(gq.at[(0,) + pair], q_recv.at[c, zt])
        pltpu.make_async_remote_copy(
            src_ref=gq.at[(0,) + pair], dst_ref=gq.at[(1,) + pair],
            send_sem=p_send, recv_sem=p_recv.at[c], device_id={"seq": mate, "head": 1},
        ).start()

    def sent(ref, sem):
        pltpu.make_async_remote_copy(
            src_ref=ref, dst_ref=ref, send_sem=sem, recv_sem=b_recv, device_id={"seq": mate},
        ).wait_send()

    for c in range(R):
        for zt in others:
            query_copy(c, 0, 2 * zt + y).start()
        query_copy(c, 1, mate).start()

        @pl.when(hr == 0)
        def _():
            query_copy(c, 0, me).start()

    @pl.when(hr == 1)
    def _():
        gq[0, own] = mine[...]

    for c in load_sel:
        c.wait()
    def groups_of(side):
        row = lax.broadcasted_iota(jnp.int32, (H, groups), 0)
        block = lax.div(row, hb)
        seq = 2 * lax.div(block, 2) + columns[side]
        head = (seq * hc + lax.rem(block, 2)) * hb + lax.rem(row, hb)
        return lax.div(head, GH) == lax.broadcasted_iota(jnp.int32, (H, groups), 1)

    tok = me * T + lax.broadcasted_iota(jnp.int32, (groups, T), 1)
    page_of = lax.div(tok, PAGE)
    tok_col = me * T + lax.broadcasted_iota(jnp.int32, (T, 1), 0)
    page_col = (me * pages + lax.broadcasted_iota(jnp.int32, (pages, 1), 0)) * PAGE
    HALF, GAP = LANES // 2, LANES // 8

    def masks():
        hot_b = [jnp.where(groups_of(side), 1.0, 0.0).astype(bf16) for side in range(2)]
        for r in range(R):
            length = len_ref[r]
            sel = sel_ref[r]
            hit = jnp.zeros((groups, T), f32)
            for k in range(sel.shape[1]):
                hit = jnp.where(sel[:, k:k + 1] == page_of, 1.0, hit)
            hit = jnp.where(tok < length, hit, 0.0).astype(bf16)
            for side in range(2):
                mask = jnp.dot(hot_b[side], hit, preferred_element_type=f32)
                pen[side, r] = (1.0 - mask) * LOWEST

    def transposed(r):
        TILE = 128 if T % 128 == 0 else T
        eye = jnp.where(
            lax.broadcasted_iota(jnp.int32, (TILE, TILE), 0)
            == lax.broadcasted_iota(jnp.int32, (TILE, TILE), 1), 1.0, 0.0
        ).astype(bf16)
        if r == 0:
            pltpu.make_async_copy(cache_hbm, cache, load_sem.at[6]).wait()
        return jnp.concatenate(
            [
                lax.dot_general(
                    eye, cache[r, :, t * TILE:(t + 1) * TILE], NT, preferred_element_type=f32
                )
                for t in range(T // TILE)
            ],
            axis=0,
        )

    def page_extremes():
        for r in range(R):
            length = len_ref[r]
            x = transposed(r)
            live = tok_col < length
            low = jnp.min(jnp.where(live, x, jnp.inf).reshape(pages, PAGE, D), axis=1)
            high = jnp.max(jnp.where(live, x, -jnp.inf).reshape(pages, PAGE, D), axis=1)
            live_page = page_col < length
            lo_s[r] = jnp.where(live_page, low, 0.0).astype(bf16)
            hi_s[r] = jnp.where(live_page, high, 0.0).astype(bf16)

    def out_span(c):
        return pl.ds(c * KT, KT + 1) if c == R - 1 else pl.ds(c * KT, KT)

    def send_out(side, c, zt):
        def out_copy(h):
            return pltpu.make_async_remote_copy(
                src_ref=so.at[side * n + 2 * zt + h, out_span(c)], dst_ref=ro.at[me, out_span(c)],
                send_sem=o_send, recv_sem=o_recv,
                device_id={"seq": 2 * zt + columns[side], "head": h},
            )

        out_copy(0).start()
        if side:
            out_copy(1).start()
        else:
            @pl.when(z != zt)
            def _():
                out_copy(1).start()

    def fill(side, c):
        at = c % PER * DR
        for j in range(n):
            rows = slice(j * hb, (j + 1) * hb)
            for k in range(KT):
                qf[side, c, rows, k * LANES:(k + 1) * LANES] = gq[
                    side, j, RT + c * KT + k
                ].astype(f32)
            qf[side, c, rows, DL:] = gq[side, j, c // PER].astype(f32)[:, at:at + DR]

    def attend(side, c, stats):
        lane = lax.broadcasted_iota(jnp.int32, (H, LANES), 1)
        fill(side, c)
        q = qf[side, c].astype(bf16)
        s = jnp.dot(q, cache[c], preferred_element_type=f32) * scale + pen[side, c]
        m = jnp.maximum(jnp.max(s, axis=1, keepdims=True), FLOOR)
        w = jnp.exp(s - m).astype(bf16)
        l = jnp.sum(w.astype(f32), axis=1, keepdims=True)
        o = jnp.dot(w, latents[c], preferred_element_type=f32)
        stats = jnp.where(lane == c, m, jnp.where(lane == HALF + c, l, stats))
        for j in range(n):
            for k in range(KT):
                so[side * n + j, c * KT + k] = o[
                    j * hb:(j + 1) * hb, k * LANES:(k + 1) * LANES
                ].astype(bf16)
        if c == R - 1:
            first = stats.astype(bf16).astype(f32)
            rest = stats - first
            second = rest.astype(bf16).astype(f32)
            third = rest - second
            packed = first + pltpu.roll(second, GAP, 1) + pltpu.roll(third, 2 * GAP, 1)
            for j in range(n):
                so[side * n + j, R * KT] = packed[j * hb:(j + 1) * hb].astype(bf16)
        return stats

    def hand_over(side):
        return pltpu.make_async_remote_copy(
            src_ref=gq.at[side], dst_ref=gq.at[side],
            send_sem=f_send, recv_sem=f_recv.at[side], device_id={"head": 0},
        )

    def find_bounds():
        best = None
        for side in range(2):
            hot = groups_of(side)
            parts = []
            hand_over(side).wait_recv()
            for r in range(R):
                fill(side, r)
                q = qf[side, r]
                above = jnp.maximum(q, 0.0).astype(bf16)
                below = jnp.minimum(q, 0.0).astype(bf16)
                parts.append(
                    lax.dot_general(above, hi_s[r], NT, preferred_element_type=f32)
                    + lax.dot_general(below, lo_s[r], NT, preferred_element_type=f32)
                )
            parts.append(jnp.zeros((H, LANES - R * pages), f32))
            head_bound = jnp.concatenate(parts, axis=1) * scale
            found = jnp.concatenate(
                [
                    jnp.max(
                        jnp.where(hot[:, g:g + 1], head_bound, LOWEST), axis=0, keepdims=True
                    )
                    for g in range(groups)
                ],
                axis=0,
            )
            best = found if best is None else jnp.maximum(best, found)
        gb[...] = best

    b_copy = pltpu.make_async_remote_copy(
        src_ref=gb, dst_ref=gbr, send_sem=b_send, recv_sem=b_recv, device_id={"head": 1},
    )

    @pl.when(hr == 1)
    def _():
        masks()
        for r in range(R):
            latents[r] = transposed(r)[:, :DL].astype(bf16)
        for side in range(2):
            stats = jnp.zeros((H, LANES), f32)
            for c in range(R):
                if side:
                    wait_for(gq.at[1, pl.ds(0, n), span(c)], p_recv.at[c])
                else:
                    for zt in reversed(others):
                        pass_on(c, zt)
                    wait_for(gq.at[0, pl.ds(2 * z, 1), span(c)], q_recv.at[c, z])
                if c == R - 1:
                    hand_over(side).start()
                stats = attend(side, c, stats)
                send_out(side, c, 0)
                for zt in range(1, nz):
                    @pl.when(zt >= z)
                    def _():
                        send_out(side, c, zt)
                if side == 0:
                    @pl.when(jnp.logical_and(y == 0, z > 1))
                    def _():
                        send_out(0, c, 1)
                if side == 0:
                    ro[me, out_span(c)] = so[2 * z + 1, out_span(c)]

        @pl.when(z > 1)
        def _():
            for c in range(R):
                send_out(1, c, 1)

        @pl.when(jnp.logical_and(y == 1, z > 1))
        def _():
            for c in range(R):
                send_out(0, c, 1)
        for side in range(2):
            for c in range(R):
                for zt in range(2, nz):
                    @pl.when(zt < z)
                    def _():
                        send_out(side, c, zt)
        b_copy.wait_recv()

    @pl.when(hr == 0)
    def _():
        page_extremes()
        find_bounds()
        b_copy.start()
        gbr[...] = gb[...]

    load_uv.wait()
    page_row = (me * pages + lax.broadcasted_iota(jnp.int32, (groups, pages), 1)) * PAGE
    best = gbr[...]
    for r in range(R):
        bounds_ref[r] = jnp.where(
            page_row < len_ref[r], best[:, r * pages:(r + 1) * pages], 0.0
        )

    def out_wait(count):
        ref = ro.at[pl.ds(0, count)]
        pltpu.make_async_remote_copy(
            src_ref=ref, dst_ref=ref, send_sem=o_send, recv_sem=o_recv, device_id={"seq": mate},
        ).wait_recv()

    pl.when(hr == 0)(lambda: out_wait(n))
    pl.when(hr == 1)(lambda: out_wait(n - 1))

    def statistics(b):
        x = ro[b, R * KT].astype(f32)
        return x + pltpu.roll(x, LANES - GAP, 1) + pltpu.roll(x, LANES - 2 * GAP, 1)

    held = [statistics(b) for b in range(n)]
    peak = held[0]
    for b in range(1, n):
        peak = jnp.maximum(peak, held[b])
    shares = [jnp.exp(x - peak) for x in held]
    total = shares[0] * pltpu.roll(held[0], HALF, 1)
    for b in range(1, n):
        total += shares[b] * pltpu.roll(held[b], HALF, 1)
    shares = [x / total for x in shares]
    rows = []
    for r in range(R):
        parts = []
        for k in range(KT):
            acc = jnp.zeros((hb, LANES), f32)
            for b in range(n):
                acc += shares[b][:, r:r + 1] * ro[b, r * KT + k].astype(f32)
            parts.append(acc)
        rows.append(jnp.concatenate(parts, axis=1))
    lhs = spread(jnp.concatenate(rows, axis=0), DL)
    res = jnp.dot(lhs, wuv[...].reshape(lhs.shape[1], wuv.shape[2]), preferred_element_type=f32)
    for r in range(R):
        out_ref[r] = res[r * hb:(r + 1) * hb].astype(bf16)

    @pl.when(hr == 1)
    def _():
        sent(gq, f_send)
        sent(gq.at[0, pl.ds(0, nz)], q_send)
        sent(gq.at[0, pl.ds(0, n - 2)], p_send)
        sent(so.at[pl.ds(0, 2 * n - 1)], o_send)

    @pl.when(hr == 0)
    def _():
        b_copy.wait_send()
        sent(gq.at[0, pl.ds(0, nz + 1)], q_send)


def local(n, hc, q_nope, q_rope, w_uk, w_uv, cache, lengths, selected):
    R, hb, DN = q_nope.shape
    DL, DV = w_uk.shape[2], w_uv.shape[2]
    T, D = cache.shape[1:]
    groups = selected.shape[1]
    pages = T // PAGE
    H = n * hb
    scale = (DN + q_rope.shape[2]) ** (-0.5)
    f32, bf16 = jnp.float32, jnp.bfloat16
    KT = DL // LANES
    tiles = R * KT - (-R // (LANES // q_rope.shape[2]))
    V = pltpu.VMEM
    vm = pl.BlockSpec(memory_space=pltpu.VMEM)
    hbm = pl.BlockSpec(memory_space=pltpu.HBM)
    dma = pltpu.SemaphoreType.DMA
    return pl.pallas_call(
        functools.partial(kernel, n, hc, R, hb, T, DL, D, groups, scale),
        out_shape=(
            V((R, hb, DV), bf16),
            V((R, groups, pages), f32),
        ),
        in_specs=[hbm] * 7,
        out_specs=(vm, vm),
        scratch_shapes=[
            pltpu.SMEM(lengths.shape, jnp.int32),
            V(q_nope.shape, bf16),
            V(q_rope.shape, bf16),
            V(selected.shape, jnp.int32),
            V((hb, DN, DL), bf16),
            V((hb, DL, DV), bf16),
            V((R, D, T), bf16),
            V((R, T, DL), bf16),
            V((tiles, hb, LANES), bf16),
            V((2, n, tiles, hb, LANES), bf16),
            V((2, R, H, D), f32),
            V((2, R, H, T), f32),
            V((R, pages, D), bf16),
            V((R, pages, D), bf16),
            V((2 * n, R * KT + 1, hb, LANES), bf16),
            V((n, R * KT + 1, hb, LANES), bf16),
            V((groups, LANES), f32),
            V((groups, LANES), f32),
            dma((7,)),
            dma, dma, dma, dma, dma,
            dma((R, n // 2)),
            dma((R,)),
            dma, dma, dma((2,)),
        ],
        compiler_params=pltpu.CompilerParams(
            collective_id=0, has_side_effects=True, vmem_limit_bytes=61000 * 1024
        ),
    )(lengths, q_nope, q_rope, selected, w_uk, w_uv, jnp.swapaxes(cache, 1, 2))


def solution(mesh):
    placed = (
        P("grp", ("seq", "head"), None),
        P("grp", ("seq", "head"), None),
        P(("seq", "head"), None, None),
        P(("seq", "head"), None, None),
        P("grp", "seq", None),
        P("grp"),
        P("grp", None, None),
    )
    return jax.shard_map(
        functools.partial(local, mesh.shape["seq"], mesh.shape["head"]),
        mesh=mesh,
        in_specs=placed,
        out_specs=(P("grp", ("seq", "head"), None), P("grp", None, "seq")),
        check_vma=False,
    )
```

```python
import functools

import jax
import jax.numpy as jnp
from jax import lax
from jax.experimental import pallas as pl
from jax.experimental.pallas import tpu as pltpu
from jax.sharding import PartitionSpec as P

GH = 16
PAGE = 64
LANES = 128
LOWEST = -1e30
FLOOR = -1e29
NT = (((1,), (1,)), ((), ()))


def kernel(
    n, hc, R, hb, T, DL, D, groups, scale,
    len_hbm, qn_hbm, qr_hbm, sel_hbm, wuk_hbm, wuv_hbm, cache_hbm,
    out_ref, bounds_ref,
    len_ref, qn_ref, qr_ref, sel_ref, wuk, wuv, cache, latents, mine, gq, qf, pen, hi_s, lo_s, so, ro, gb, gbr,
    load_sem, q_send, p_send, o_send, b_send, f_send, q_recv, p_recv, o_recv, b_recv, f_recv,
):
    f32, bf16 = jnp.float32, jnp.bfloat16
    me = lax.axis_index("seq")
    hr = lax.axis_index("head")
    H = n * hb
    DR = D - DL
    KT = DL // LANES
    PER = LANES // DR
    RT = -(-R // PER)
    pages = T // PAGE
    nz = n // 2
    z = lax.div(me, 2)
    y = lax.rem(me, 2)
    mate = me + 1 - 2 * y
    columns = (y, 1 - y)
    low_half = 2 * z < nz

    def other(i):
        down = nz - 1 - i
        down = jnp.where(down <= z, down - 1, down)
        up = jnp.where(z <= i, i + 1, i)
        return jnp.where(low_half, down, up)

    others = [other(i) for i in range(nz - 1)]

    load_uk = [
        pltpu.make_async_copy(wuk_hbm.at[h], wuk.at[h], load_sem.at[0 if 2 * h < hb else 7]) for h in range(hb)
    ]
    load_cache = [
        pltpu.make_async_copy(cache_hbm.at[r], cache.at[r], load_sem.at[6]) for r in range(R)
    ]
    load_uv = pltpu.make_async_copy(wuv_hbm, wuv, load_sem.at[1])
    load_q = [
        pltpu.make_async_copy(qn_hbm, qn_ref, load_sem.at[2]),
        pltpu.make_async_copy(qr_hbm, qr_ref, load_sem.at[3]),
    ]
    load_sel = [
        pltpu.make_async_copy(sel_hbm, sel_ref, load_sem.at[4]),
        pltpu.make_async_copy(len_hbm, len_ref, load_sem.at[5]),
    ]

    barrier = pltpu.get_barrier_semaphore()

    @pl.when(hr == 1)
    def _():
        for seq in [2 * zt + y for zt in others] + [mate]:
            for h in range(hc):
                pl.semaphore_signal(barrier, inc=1, device_id={"seq": seq, "head": h})
        pl.semaphore_signal(barrier, inc=1, device_id={"head": 0})

    for c in load_q + load_uk + load_sel:
        c.start()

    def spread(rows, width):
        which = lax.rem(lax.broadcasted_iota(jnp.int32, (R * hb, width), 0), hb)
        return jnp.concatenate(
            [jnp.where(which == h, rows, 0.0).astype(bf16) for h in range(hb)], axis=1
        )

    for c in load_q:
        c.wait()
    for t in range(RT):
        parts = [qr_ref[r].astype(f32) for r in range(t * PER, min(R, (t + 1) * PER))]
        parts += [jnp.zeros((hb, DR), f32)] * (PER - len(parts))
        mine[t] = jnp.concatenate(parts, axis=1).astype(bf16)
    qn = jnp.concatenate([qn_ref[r].astype(f32) for r in range(R)], axis=0)
    lhs = spread(qn, qn.shape[1])
    DN = qn.shape[1]
    half = hb // 2
    latent = None
    for first, sem in ((0, 0), (half, 7)):
        part = pl.ds(first, half)
        pltpu.make_async_copy(wuk_hbm.at[part], wuk.at[part], load_sem.at[sem]).wait()
        more = jnp.dot(
            lhs[:, first * DN:(first + half) * DN], wuk[part].reshape(half * DN, DL),
            preferred_element_type=f32,
        )
        latent = more if latent is None else latent + more
    for c in load_cache:
        c.start()
    load_uv.start()
    for r in range(R):
        for k in range(KT):
            mine[RT + r * KT + k] = latent[
                r * hb:(r + 1) * hb, k * LANES:(k + 1) * LANES
            ].astype(bf16)

    pl.semaphore_wait(barrier, nz + 1 - hr)

    def span(c):
        return pl.ds(RT + c * KT, KT) if c else pl.ds(0, RT + KT)

    own = 2 * z + hr

    def query_copy(c, side, seq):
        return pltpu.make_async_remote_copy(
            src_ref=mine.at[span(c)], dst_ref=gq.at[side, own, span(c)],
            send_sem=q_send, recv_sem=p_recv.at[c] if side else q_recv.at[c, z],
            device_id={"seq": seq, "head": 1},
        )

    def wait_for(ref, sem):
        pltpu.make_async_remote_copy(
            src_ref=ref, dst_ref=ref, send_sem=q_send, recv_sem=sem, device_id={"seq": mate},
        ).wait_recv()

    def pass_on(c, zt):
        pair = (pl.ds(2 * zt, 2), span(c))
        wait_for(gq.at[(0,) + pair], q_recv.at[c, zt])
        pltpu.make_async_remote_copy(
            src_ref=gq.at[(0,) + pair], dst_ref=gq.at[(1,) + pair],
            send_sem=p_send, recv_sem=p_recv.at[c], device_id={"seq": mate, "head": 1},
        ).start()

    def sent(ref, sem):
        pltpu.make_async_remote_copy(
            src_ref=ref, dst_ref=ref, send_sem=sem, recv_sem=b_recv, device_id={"seq": mate},
        ).wait_send()

    for c in range(R):
        for zt in others:
            query_copy(c, 0, 2 * zt + y).start()
        query_copy(c, 1, mate).start()

        @pl.when(hr == 0)
        def _():
            query_copy(c, 0, me).start()

    @pl.when(hr == 1)
    def _():
        gq[0, own] = mine[...]

    for c in load_sel:
        c.wait()
    def groups_of(side):
        row = lax.broadcasted_iota(jnp.int32, (H, groups), 0)
        block = lax.div(row, hb)
        seq = 2 * lax.div(block, 2) + columns[side]
        head = (seq * hc + lax.rem(block, 2)) * hb + lax.rem(row, hb)
        return lax.div(head, GH) == lax.broadcasted_iota(jnp.int32, (H, groups), 1)

    tok = me * T + lax.broadcasted_iota(jnp.int32, (groups, T), 1)
    page_of = lax.div(tok, PAGE)
    tok_col = me * T + lax.broadcasted_iota(jnp.int32, (T, 1), 0)
    page_col = (me * pages + lax.broadcasted_iota(jnp.int32, (pages, 1), 0)) * PAGE
    HALF, GAP = LANES // 2, LANES // 8

    def masks():
        hot_b = [jnp.where(groups_of(side), 1.0, 0.0).astype(bf16) for side in range(2)]
        for r in range(R):
            length = len_ref[r]
            sel = sel_ref[r]
            hit = jnp.zeros((groups, T), f32)
            for k in range(sel.shape[1]):
                hit = jnp.where(sel[:, k:k + 1] == page_of, 1.0, hit)
            hit = jnp.where(tok < length, hit, 0.0).astype(bf16)
            for side in range(2):
                mask = jnp.dot(hot_b[side], hit, preferred_element_type=f32)
                pen[side, r] = (1.0 - mask) * LOWEST

    def transposed(r):
        TILE = 128 if T % 128 == 0 else T
        eye = jnp.where(
            lax.broadcasted_iota(jnp.int32, (TILE, TILE), 0)
            == lax.broadcasted_iota(jnp.int32, (TILE, TILE), 1), 1.0, 0.0
        ).astype(bf16)
        if r == 0:
            pltpu.make_async_copy(cache_hbm, cache, load_sem.at[6]).wait()
        return jnp.concatenate(
            [
                lax.dot_general(
                    eye, cache[r, :, t * TILE:(t + 1) * TILE], NT, preferred_element_type=f32
                )
                for t in range(T // TILE)
            ],
            axis=0,
        )

    def page_extremes():
        for r in range(R):
            length = len_ref[r]
            x = transposed(r)
            live = tok_col < length
            low = jnp.min(jnp.where(live, x, jnp.inf).reshape(pages, PAGE, D), axis=1)
            high = jnp.max(jnp.where(live, x, -jnp.inf).reshape(pages, PAGE, D), axis=1)
            live_page = page_col < length
            lo_s[r] = jnp.where(live_page, low, 0.0).astype(bf16)
            hi_s[r] = jnp.where(live_page, high, 0.0).astype(bf16)

    def out_span(c):
        return pl.ds(c * KT, KT + 1) if c == R - 1 else pl.ds(c * KT, KT)

    def send_out(side, c, zt):
        def out_copy(h):
            return pltpu.make_async_remote_copy(
                src_ref=so.at[side * n + 2 * zt + h, out_span(c)], dst_ref=ro.at[me, out_span(c)],
                send_sem=o_send, recv_sem=o_recv,
                device_id={"seq": 2 * zt + columns[side], "head": h},
            )

        out_copy(0).start()
        if side:
            out_copy(1).start()
        else:
            @pl.when(z != zt)
            def _():
                out_copy(1).start()

    def fill(side, c):
        at = c % PER * DR
        for j in range(n):
            rows = slice(j * hb, (j + 1) * hb)
            for k in range(KT):
                qf[side, c, rows, k * LANES:(k + 1) * LANES] = gq[
                    side, j, RT + c * KT + k
                ].astype(f32)
            qf[side, c, rows, DL:] = gq[side, j, c // PER].astype(f32)[:, at:at + DR]

    def attend(side, c, stats):
        lane = lax.broadcasted_iota(jnp.int32, (H, LANES), 1)
        fill(side, c)
        q = qf[side, c].astype(bf16)
        s = jnp.dot(q, cache[c], preferred_element_type=f32) * scale + pen[side, c]
        m = jnp.maximum(jnp.max(s, axis=1, keepdims=True), FLOOR)
        w = jnp.exp(s - m).astype(bf16)
        l = jnp.sum(w.astype(f32), axis=1, keepdims=True)
        o = jnp.dot(w, latents[c], preferred_element_type=f32)
        stats = jnp.where(lane == c, m, jnp.where(lane == HALF + c, l, stats))
        for j in range(n):
            for k in range(KT):
                so[side * n + j, c * KT + k] = o[
                    j * hb:(j + 1) * hb, k * LANES:(k + 1) * LANES
                ].astype(bf16)
        if c == R - 1:
            first = stats.astype(bf16).astype(f32)
            rest = stats - first
            second = rest.astype(bf16).astype(f32)
            third = rest - second
            packed = first + pltpu.roll(second, GAP, 1) + pltpu.roll(third, 2 * GAP, 1)
            for j in range(n):
                so[side * n + j, R * KT] = packed[j * hb:(j + 1) * hb].astype(bf16)
        return stats

    def hand_over(side):
        return pltpu.make_async_remote_copy(
            src_ref=gq.at[side], dst_ref=gq.at[side],
            send_sem=f_send, recv_sem=f_recv.at[side], device_id={"head": 0},
        )

    def find_bounds():
        best = None
        for side in range(2):
            hot = groups_of(side)
            parts = []
            hand_over(side).wait_recv()
            for r in range(R):
                fill(side, r)
                q = qf[side, r]
                above = jnp.maximum(q, 0.0).astype(bf16)
                below = jnp.minimum(q, 0.0).astype(bf16)
                parts.append(
                    lax.dot_general(above, hi_s[r], NT, preferred_element_type=f32)
                    + lax.dot_general(below, lo_s[r], NT, preferred_element_type=f32)
                )
            parts.append(jnp.zeros((H, LANES - R * pages), f32))
            head_bound = jnp.concatenate(parts, axis=1) * scale
            found = jnp.concatenate(
                [
                    jnp.max(
                        jnp.where(hot[:, g:g + 1], head_bound, LOWEST), axis=0, keepdims=True
                    )
                    for g in range(groups)
                ],
                axis=0,
            )
            best = found if best is None else jnp.maximum(best, found)
        gb[...] = best

    b_copy = pltpu.make_async_remote_copy(
        src_ref=gb, dst_ref=gbr, send_sem=b_send, recv_sem=b_recv, device_id={"head": 1},
    )

    @pl.when(hr == 1)
    def _():
        masks()
        for r in range(R):
            latents[r] = transposed(r)[:, :DL].astype(bf16)
        for side in range(2):
            stats = jnp.zeros((H, LANES), f32)
            for c in range(R):
                if side:
                    wait_for(gq.at[1, pl.ds(0, n), span(c)], p_recv.at[c])
                else:
                    for zt in reversed(others):
                        pass_on(c, zt)
                    wait_for(gq.at[0, pl.ds(2 * z, 1), span(c)], q_recv.at[c, z])
                if c == R - 1:
                    hand_over(side).start()
                stats = attend(side, c, stats)
                send_out(side, c, 0)
                for zt in range(1, nz):
                    @pl.when(zt >= z)
                    def _():
                        send_out(side, c, zt)
                if side == 0:
                    @pl.when(jnp.logical_and(y == 0, z > 1))
                    def _():
                        send_out(0, c, 1)
                if side == 0:
                    ro[me, out_span(c)] = so[2 * z + 1, out_span(c)]

        @pl.when(z > 1)
        def _():
            for c in range(R):
                send_out(1, c, 1)

        @pl.when(jnp.logical_and(y == 1, z > 1))
        def _():
            for c in range(R):
                send_out(0, c, 1)
        for side in range(2):
            for c in range(R):
                for zt in range(2, nz):
                    @pl.when(zt < z)
                    def _():
                        send_out(side, c, zt)
        b_copy.wait_recv()

    @pl.when(hr == 0)
    def _():
        page_extremes()
        find_bounds()
        b_copy.start()
        gbr[...] = gb[...]

    load_uv.wait()
    page_row = (me * pages + lax.broadcasted_iota(jnp.int32, (groups, pages), 1)) * PAGE
    best = gbr[...]
    for r in range(R):
        bounds_ref[r] = jnp.where(
            page_row < len_ref[r], best[:, r * pages:(r + 1) * pages], 0.0
        )

    def out_wait(count):
        ref = ro.at[pl.ds(0, count)]
        pltpu.make_async_remote_copy(
            src_ref=ref, dst_ref=ref, send_sem=o_send, recv_sem=o_recv, device_id={"seq": mate},
        ).wait_recv()

    pl.when(hr == 0)(lambda: out_wait(n))
    pl.when(hr == 1)(lambda: out_wait(n - 1))

    def statistics(b):
        x = ro[b, R * KT].astype(f32)
        return x + pltpu.roll(x, LANES - GAP, 1) + pltpu.roll(x, LANES - 2 * GAP, 1)

    held = [statistics(b) for b in range(n)]
    peak = held[0]
    for b in range(1, n):
        peak = jnp.maximum(peak, held[b])
    shares = [jnp.exp(x - peak) for x in held]
    total = shares[0] * pltpu.roll(held[0], HALF, 1)
    for b in range(1, n):
        total += shares[b] * pltpu.roll(held[b], HALF, 1)
    shares = [x / total for x in shares]
    rows = []
    for r in range(R):
        parts = []
        for k in range(KT):
            acc = jnp.zeros((hb, LANES), f32)
            for b in range(n):
                acc += shares[b][:, r:r + 1] * ro[b, r * KT + k].astype(f32)
            parts.append(acc)
        rows.append(jnp.concatenate(parts, axis=1))
    lhs = spread(jnp.concatenate(rows, axis=0), DL)
    res = jnp.dot(lhs, wuv[...].reshape(lhs.shape[1], wuv.shape[2]), preferred_element_type=f32)
    for r in range(R):
        out_ref[r] = res[r * hb:(r + 1) * hb].astype(bf16)

    @pl.when(hr == 1)
    def _():
        sent(gq, f_send)
        sent(gq.at[0, pl.ds(0, nz)], q_send)
        sent(gq.at[0, pl.ds(0, n - 2)], p_send)
        sent(so.at[pl.ds(0, 2 * n - 1)], o_send)

    @pl.when(hr == 0)
    def _():
        b_copy.wait_send()
        sent(gq.at[0, pl.ds(0, nz + 1)], q_send)


def local(n, hc, q_nope, q_rope, w_uk, w_uv, cache, lengths, selected):
    R, hb, DN = q_nope.shape
    DL, DV = w_uk.shape[2], w_uv.shape[2]
    T, D = cache.shape[1:]
    groups = selected.shape[1]
    pages = T // PAGE
    H = n * hb
    scale = (DN + q_rope.shape[2]) ** (-0.5)
    f32, bf16 = jnp.float32, jnp.bfloat16
    KT = DL // LANES
    tiles = R * KT - (-R // (LANES // q_rope.shape[2]))
    V = pltpu.VMEM
    vm = pl.BlockSpec(memory_space=pltpu.VMEM)
    hbm = pl.BlockSpec(memory_space=pltpu.HBM)
    dma = pltpu.SemaphoreType.DMA
    return pl.pallas_call(
        functools.partial(kernel, n, hc, R, hb, T, DL, D, groups, scale),
        out_shape=(
            V((R, hb, DV), bf16),
            V((R, groups, pages), f32),
        ),
        in_specs=[hbm] * 7,
        out_specs=(vm, vm),
        scratch_shapes=[
            pltpu.SMEM(lengths.shape, jnp.int32),
            V(q_nope.shape, bf16),
            V(q_rope.shape, bf16),
            V(selected.shape, jnp.int32),
            V((hb, DN, DL), bf16),
            V((hb, DL, DV), bf16),
            V((R, D, T), bf16),
            V((R, T, DL), bf16),
            V((tiles, hb, LANES), bf16),
            V((2, n, tiles, hb, LANES), bf16),
            V((2, R, H, D), f32),
            V((2, R, H, T), f32),
            V((R, pages, D), bf16),
            V((R, pages, D), bf16),
            V((2 * n, R * KT + 1, hb, LANES), bf16),
            V((n, R * KT + 1, hb, LANES), bf16),
            V((groups, LANES), f32),
            V((groups, LANES), f32),
            dma((8,)),
            dma, dma, dma, dma, dma,
            dma((R, n // 2)),
            dma((R,)),
            dma, dma, dma((2,)),
        ],
        compiler_params=pltpu.CompilerParams(
            collective_id=0, has_side_effects=True, vmem_limit_bytes=61000 * 1024
        ),
    )(lengths, q_nope, q_rope, selected, w_uk, w_uv, jnp.swapaxes(cache, 1, 2))


def solution(mesh):
    placed = (
        P("grp", ("seq", "head"), None),
        P("grp", ("seq", "head"), None),
        P(("seq", "head"), None, None),
        P(("seq", "head"), None, None),
        P("grp", "seq", None),
        P("grp"),
        P("grp", None, None),
    )
    return jax.shard_map(
        functools.partial(local, mesh.shape["seq"], mesh.shape["head"]),
        mesh=mesh,
        in_specs=placed,
        out_specs=(P("grp", ("seq", "head"), None), P("grp", None, "seq")),
        check_vma=False,
    )
```
